128 devices in a mesh: gx: 8 (over x, core), gy: 16 (over y, z).
Axes of the slice: x: 4, y: 4, z: 4, core: 2. Of those that a mesh axis runs over, the one named last changes fastest.
Arguments:
- coil_images: float32 [2, 2, 512, 256, 256], P(None, None, 'gx', 'gy'), may hold values from -6 to 6
- send_lists: int32 [128, 128, 4], P(('gx', 'gy')), may hold values from -1 to 65535, as said below
- seg_slots: int32 [2048, 16], P(('gx', 'gy')), may hold values from 0 to 511, as said below
- weights: float32 [2048, 16, 16, 512], P(('gx', 'gy')), may hold values from -0.0625 to 0.0625
- counts: int32 [2048], P(('gx', 'gy')), may hold values from 1 to 16
Outputs:
- kspace: float32 [2048, 2, 2, 16], P(('gx', 'gy'))
The draws below stay inside these ranges and needn't reach their ends.
Inputs may be any that keep to these rules, and one draw needn't show every extreme that they name: Every entry of send_lists[d] that is not -1 names a grid block held by device d, with devices numbered x slab first: the block's x cells lie in device d's x cells and its y cells in device d's y cells. seg_slots[s, l] = j * 4 + k always names a slot with send_lists[j, s // 16, k] >= 0; the slots named by the segments of one owner are distinct, and every used slot of send_lists is named once.
All inputs are finite; a program needn't handle non-finite values.
Results may differ from the reference program's by a relative error of at most 0.00011.
Values sent between devices are 32-bit elements; how exact they have to be, the bound alone decides.
A program may use at most 256 MiB of HBM per device.

```python
import math
import jax
import jax.numpy as jnp
from jax import lax

NX = 512
NY = 256
NZ = 256
COILS = 2
BLOCK = 8
SEG_DEV = 16
LIST = 16
SAMP = 16
SEGS = 2048
CAP = 4
CELLS = 512
MY = 16
MBX = 8
MBY = 2
NBY = 32
NBZ = 32
NBLOCKS = 65536
DEVICES = 128


def build_plan(key):
    devices = DEVICES
    entries = SEG_DEV * LIST
    slot_count = devices * CAP
    y_devices = NY // MY
    key_full = jax.random.fold_in(key, 71)
    key_perm = jax.random.fold_in(key, 72)
    key_reorder = jax.random.fold_in(key, 73)
    key_local = jax.random.fold_in(key, 74)
    full_source = jax.random.randint(key_full, (devices,), 0, devices)
    slot_source = jnp.arange(slot_count, dtype=jnp.int32) // CAP

    def choose(owner):
        shuffled = jax.random.permutation(jax.random.fold_in(key_perm, owner), slot_count)
        slot_rank = jnp.argsort(shuffled, stable=True).astype(jnp.int32)
        priority = jnp.where(slot_source == full_source[owner], -1, slot_rank)
        chosen = jnp.argsort(priority, stable=True)[:entries].astype(jnp.int32)
        reorder = jax.random.permutation(jax.random.fold_in(key_reorder, owner), entries)
        return chosen[reorder]
    owner_list = jnp.arange(devices, dtype=jnp.int32)
    chosen_all = jax.vmap(choose)(owner_list)
    slot_used = jnp.zeros((devices, slot_count), jnp.int32).at[owner_list[:, None], chosen_all].set(1)
    slot_used = slot_used.reshape(devices, devices, CAP).transpose(1, 0, 2)
    local_id = jax.random.randint(key_local, (devices, devices, CAP), 0, MBX * MBY * NBZ)
    sender = jnp.arange(devices, dtype=jnp.int32)[:, None, None]
    block_x = sender // y_devices * MBX + local_id // (MBY * NBZ)
    block_y = sender % y_devices * MBY + local_id // NBZ % MBY
    block_z = local_id % NBZ
    global_id = (block_x * NBY + block_y) * NBZ + block_z
    send_lists = jnp.where(slot_used > 0, global_id, -1).astype(jnp.int32)
    seg_slots = chosen_all.reshape(devices * SEG_DEV, LIST).astype(jnp.int32)
    return (send_lists, seg_slots)


def draw_send_lists(key, part):
    return build_plan(key)[0]


def draw_seg_slots(key, part):
    return build_plan(key)[1]


def place_ends(result, own_key, least, high):
    shape = result.shape
    index_at = [jax.random.randint(jax.random.fold_in(own_key, axis), (), 0, shape[axis]) for axis in range(len(shape))]
    result = result.at[tuple(index_at)].set(least)
    longest = shape.index(max(shape))
    index_at[longest] = (index_at[longest] + 1) % shape[longest]
    return result.at[tuple(index_at)].set(high)


def block_scale(rng, dims, cuts, low, top_value):
    gain = 1.0
    for axis_at, blocks in cuts:
        draws = jax.random.uniform(jax.random.fold_in(jax.random.fold_in(rng, 6), axis_at), (blocks,), jnp.float32, low / len(cuts), top_value / len(cuts))
        gain = gain * jnp.repeat(jnp.exp(draws), dims[axis_at] // blocks).reshape((-1,) + (1,) * (len(dims) - 1 - axis_at))
    return gain


def centred(stream_key, extent, deviation, most, shards=(), held_as=jnp.bfloat16):
    array = jax.random.normal(stream_key, extent, jnp.float32) * deviation
    if len(shards) > 0:
        array = block_scale(stream_key, extent, shards, -0.22, 0.18) * array
    return jnp.clip(array, min=-most, max=most).astype(held_as)


def setup_inputs(seed: int = 0) -> dict:
    arg_keys = jax.random.split(jax.random.key(seed), 6)
    return {
        "coil_images": centred(arg_keys[0], (COILS, 2, NX, NY, NZ), 1.0, 6.0, ((2, 8), (3, 16)), jnp.float32),
        "send_lists": draw_send_lists(jax.random.fold_in(arg_keys[5], 71), 0),
        "seg_slots": draw_seg_slots(jax.random.fold_in(arg_keys[5], 71), 0),
        "weights": centred(arg_keys[3], (SEGS, LIST, SAMP, CELLS), (LIST * CELLS) ** -0.5, 0.0625, ((0, 128),), jnp.float32),
        "counts": place_ends(jax.random.randint(arg_keys[4], (SEGS,), 1, SAMP + 1), jax.random.fold_in(arg_keys[4], 1), 1, SAMP).astype(jnp.int32),
    }


def reference(coil_images, send_lists, seg_slots, weights, counts):
    complex_image = coil_images[:, 0] + 1j * coil_images[:, 1]
    transformed = jnp.fft.fftn(complex_image, axes=(1, 2, 3)) * (1.0 / math.sqrt(NX * NY * NZ))
    spectrum = jnp.stack([jnp.real(transformed), jnp.imag(transformed)], 1).astype(jnp.float32)
    blocks = spectrum.reshape(COILS, 2, NX // BLOCK, BLOCK, NY // BLOCK, BLOCK, NZ // BLOCK, BLOCK)
    blocks = blocks.transpose(2, 4, 6, 0, 1, 3, 5, 7).reshape(NBLOCKS, COILS * 2 * CELLS)
    owner_device = jnp.arange(SEGS, dtype=jnp.int32) // SEG_DEV
    source_device = seg_slots // CAP
    slot_pos = seg_slots % CAP
    block_ids = send_lists[source_device, owner_device[:, None], slot_pos]
    block_rows = blocks[block_ids].reshape(SEGS, LIST, COILS * 2, CELLS)
    samples = jnp.einsum('slnk,slqk->sqn', weights, block_rows, precision=lax.Precision.HIGHEST)
    live_mask = jnp.arange(SAMP, dtype=jnp.int32)[None, None, :] < counts[:, None, None]
    samples = jnp.where(live_mask, samples, jnp.zeros_like(samples))
    return samples.reshape(SEGS, COILS, 2, SAMP)
```

```python
import functools
import math

import jax
import jax.numpy as jnp
import numpy as np
from jax import lax
from jax.experimental import pallas as pl
from jax.experimental.pallas import tpu as pltpu
from jax.sharding import PartitionSpec as P

NX, NY, NZ = 512, 256, 256
GX, GY = 8, 16
DEVS = GX * GY
F32, BF16 = jnp.float32, jnp.bfloat16
VMEM_LIMIT = 48 * 2**20


def split_table(table):
    hi = table.astype(np.float32).astype(jnp.bfloat16)
    lo = (table - hi.astype(np.float64)).astype(np.float32).astype(jnp.bfloat16)
    return hi, lo


def angle(rows, columns, length):
    return (np.outer(rows, columns) % length) * (2.0 * math.pi / length)


def z_table():
    order = (np.arange(8)[:, None] + 8 * np.arange(32)[None, :]).reshape(-1)
    phase = angle(order, np.arange(NZ), NZ)
    scale = 1.0 / math.sqrt(NX * NY * NZ)
    return split_table(np.concatenate([np.cos(phase), np.sin(phase)], 1) * scale)


def x_table():
    phase = angle(np.arange(NX), np.arange(NX), NX)
    cos, sin = np.cos(phase), np.sin(phase)
    whole = np.zeros((2, NX, 2, NX))
    whole[0, :, 0], whole[1, :, 0] = cos, sin
    whole[0, :, 1], whole[1, :, 1] = -sin, cos
    whole = whole.reshape(2, 8, 64, 2, 64, 8).transpose(1, 0, 2, 5, 3, 4)
    return split_table(whole.reshape(1024, 1024))


def y_table():
    phase = angle(np.arange(NY), np.arange(NY), NY)
    return split_table(np.concatenate([np.cos(phase), np.sin(phase)], 1))


def halves(value):
    hi = value.astype(BF16)
    return hi, (value - hi.astype(F32)).astype(BF16)


def dot3(left, right, dims):
    def one(a, b):
        return lax.dot_general(a, b, (dims, ((), ())), preferred_element_type=F32)

    return one(left[0], right[0]) + (one(left[0], right[1]) + one(left[1], right[0]))


def z_kernel(near, far, hi, lo, out):
    def pair(yp, carry):
        rows, swapped = [], []
        for k in range(2):
            at = pl.ds(2 * yp + k, 64, stride=16)
            re, im = (jnp.concatenate([near[0, q, at, :], far[0, q, at, :]], 1) for q in range(2))
            rows += [re, im]
            swapped += [im, -re]
        data = jnp.concatenate(
            [jnp.concatenate(rows, 0), jnp.concatenate(swapped, 0)], 1
        )
        res = dot3((hi[...], lo[...]), halves(data), ((1,), (1,)))
        for k in range(2):
            out[:, 0, 2 * yp + k] = res[:, k * 128 : (k + 1) * 128].reshape(8, 32, 128)
        return carry

    lax.fori_loop(0, 8, pair, 0)


def z_transform(images):
    images = images.reshape(2, 2, 1024, 256)
    hi, lo = z_table()
    whole = pl.BlockSpec((256, 512), lambda c: (0, 0))
    return pl.pallas_call(
        z_kernel,
        out_shape=jax.ShapeDtypeStruct((8, 2, 16, 32, 128), F32),
        grid=(2,),
        in_specs=[
            pl.BlockSpec((1, 2, 1024, 128), lambda c: (c, 0, 0, 0)),
            pl.BlockSpec((1, 2, 1024, 128), lambda c: (c, 0, 0, 1)),
            whole,
            whole,
        ],
        out_specs=pl.BlockSpec((8, 1, 16, 32, 128), lambda c: (0, c, 0, 0, 0)),
        compiler_params=pltpu.CompilerParams(vmem_limit_bytes=VMEM_LIMIT),
        name="z_transform",
    )(images, images, jnp.asarray(hi), jnp.asarray(lo))


def x_kernel(data, hi, lo, out):
    rows = jnp.concatenate([data[a] for a in range(8)], 1)
    res = dot3(halves(rows), (hi[...], lo[...]), ((1,), (0,)))
    for u in range(8):
        out[u] = res[:, u * 128 : (u + 1) * 128]


def x_transform(data):
    hi, lo = x_table()
    whole = pl.BlockSpec((1024, 1024), lambda r: (0, 0))
    return pl.pallas_call(
        x_kernel,
        out_shape=jax.ShapeDtypeStruct((16, 512, 128), F32),
        grid=(4,),
        in_specs=[pl.BlockSpec((8, 256, 128), lambda r: (0, r, 0)), whole, whole],
        out_specs=pl.BlockSpec((8, 256, 128), lambda r: (r // 2, r % 2, 0)),
        compiler_params=pltpu.CompilerParams(vmem_limit_bytes=VMEM_LIMIT),
        name="x_transform",
    )(data, jnp.asarray(hi), jnp.asarray(lo))


def y_kernel(data, hi, lo, out):
    flat = data.reshape(2048, 128)
    sign = jnp.where(lax.broadcasted_iota(jnp.int32, (256, 128), 1) < 64, 1.0, -1.0)

    def pair(p, carry):
        rows, swapped = [], []
        for k in range(2):
            part = flat[pl.ds(2 * p + k, 256, stride=8), :]
            rows.append(part)
            swapped.append(pltpu.roll(part, 64, 1) * sign)
        both = jnp.concatenate(
            [jnp.concatenate(rows, 1), jnp.concatenate(swapped, 1)], 0
        )
        res = dot3((hi[...], lo[...]), halves(both), ((1,), (0,)))
        for k in range(2):
            out[:, 2 * p + k] = res[:, k * 128 : (k + 1) * 128].reshape(32, 8, 128)
        return carry

    lax.fori_loop(0, 4, pair, 0)


def y_transform(data):
    hi, lo = y_table()
    whole = pl.BlockSpec((256, 512), lambda g: (0, 0))
    return pl.pallas_call(
        y_kernel,
        out_shape=jax.ShapeDtypeStruct((32, 32, 8, 128), F32),
        grid=(4,),
        in_specs=[pl.BlockSpec((256, 8, 128), lambda g: (0, g, 0)), whole, whole],
        out_specs=pl.BlockSpec((32, 8, 8, 128), lambda g: (0, g, 0, 0)),
        compiler_params=pltpu.CompilerParams(vmem_limit_bytes=VMEM_LIMIT),
        name="y_transform",
    )(data.reshape(256, 32, 128), jnp.asarray(hi), jnp.asarray(lo))


def pick_kernel(ids, table, out):
    lane = jnp.bitwise_and(lax.broadcasted_iota(jnp.int32, (8, 128), 1), 63)

    def group(t, carry):
        chains = [None] * 4
        for i in range(64):
            block = ids[t * 64 + i]
            tile = table[jnp.bitwise_and(block, 1023)]
            shift = jnp.bitwise_and(i - jnp.right_shift(block, 10), 127)
            moved = pltpu.roll(tile, shift, 1)
            old = chains[i % 4]
            chains[i % 4] = moved if old is None else jnp.where(lane == i, moved, old)
        low = jnp.bitwise_and(lane, 3)
        out[t] = jnp.where(
            low < 2,
            jnp.where(low == 0, chains[0], chains[1]),
            jnp.where(low == 2, chains[2], chains[3]),
        )
        return carry

    lax.fori_loop(0, 32, group, 0)


def pick(ids, table):
    return pl.pallas_call(
        pick_kernel,
        out_shape=jax.ShapeDtypeStruct((512, 8, 128), F32),
        grid=(16,),
        in_specs=[
            pl.BlockSpec((2048,), lambda g: (g,), memory_space=pltpu.SMEM),
            pl.BlockSpec((1024, 8, 128), lambda g: (0, 0, 0)),
        ],
        out_specs=pl.BlockSpec((32, 8, 128), lambda g: (g, 0, 0)),
        compiler_params=pltpu.CompilerParams(vmem_limit_bytes=VMEM_LIMIT),
        name="pick",
    )(ids, table.reshape(1024, 8, 128))


def turn_kernel(weights, out):
    def one(n, carry):
        out[0, n] = weights[0, pl.ds(n, 128, stride=16), :].T
        return carry

    lax.fori_loop(0, 16, one, 0)


def turn_weights(weights):
    return pl.pallas_call(
        turn_kernel,
        out_shape=jax.ShapeDtypeStruct((2, 16, 512, 128), F32),
        grid=(2, 4),
        in_specs=[pl.BlockSpec((1, 2048, 128), lambda h, e: (h, 0, e))],
        out_specs=pl.BlockSpec((1, 16, 128, 128), lambda h, e: (h, 0, e, 0)),
        compiler_params=pltpu.CompilerParams(vmem_limit_bytes=VMEM_LIMIT),
        name="turn_weights",
    )(weights.reshape(2, 2048, 512))


def sum_kernel(got, weights, out):
    low = lax.broadcasted_iota(jnp.int32, (8, 128), 1) < 64

    def one(t, carry):
        w, u = t // 8, t % 8
        values = []
        for c in range(2):
            first, second = got[w, c, u, 0], got[w, c, u, 1]
            values.append(jnp.where(low, first, pltpu.roll(second, 64, 1)))
            values.append(jnp.where(low, pltpu.roll(first, 64, 1), second))
        sums = list(carry)
        for n in range(4):
            factor = weights[0, n, pl.ds(u * 64 + w, 8, stride=8), :]
            for k in range(4):
                sums[n * 4 + k] = sums[n * 4 + k] + factor * values[k]
        return tuple(sums)

    sums = lax.fori_loop(0, 64, one, (jnp.zeros((8, 128), F32),) * 16)
    rows = [jnp.sum(s, 0, keepdims=True) for s in sums]
    out[0, 0] = jnp.concatenate(rows, 0)


def interpolate(got, weights):
    return pl.pallas_call(
        sum_kernel,
        out_shape=jax.ShapeDtypeStruct((2, 4, 16, 128), F32),
        grid=(2, 4),
        in_specs=[
            pl.BlockSpec((8, 2, 8, 2, 8, 128), lambda h, n: (0, 0, 0, h, 0, 0)),
            pl.BlockSpec((1, 4, 512, 128), lambda h, n: (h, n, 0, 0)),
        ],
        out_specs=pl.BlockSpec((1, 1, 16, 128), lambda h, n: (h, n, 0, 0)),
        compiler_params=pltpu.CompilerParams(vmem_limit_bytes=VMEM_LIMIT),
        name="interpolate",
    )(got, weights)


def block_ids(send_lists, seg_slots):
    both = ("gx", "gy")
    lists = lax.all_to_all(send_lists[0], both, 0, 0, tiled=True).reshape(1, 512)
    hit = seg_slots.reshape(256, 1) == jnp.arange(512, dtype=jnp.int32)[None, :]
    ids = jnp.sum(jnp.where(hit, lists, 0), 1)
    return lax.all_gather(ids, both, axis=0, tiled=True)


def local(coil_images, send_lists, seg_slots, weights, counts):
    ids = block_ids(send_lists, seg_slots)
    turned = turn_weights(weights)
    spectrum = z_transform(coil_images).reshape(8, 1024, 128)
    spectrum = lax.all_to_all(spectrum, "gx", 0, 0, tiled=True)
    spectrum = x_transform(spectrum)
    spectrum = lax.all_to_all(spectrum, "gy", 0, 0, tiled=True)
    table = y_transform(spectrum)
    sent = pick(ids, table).reshape(128, 4, 8, 128)
    got = lax.all_to_all(sent, ("gx", "gy"), 0, 0, tiled=True)
    sums = interpolate(got.reshape(8, 2, 8, 4, 8, 128), turned)
    sums = sums.reshape(2, 16, 2, 2, 8, 16).sum(-1)
    samples = sums.transpose(0, 4, 2, 3, 1).reshape(16, 2, 2, 16)
    live = jnp.arange(16, dtype=jnp.int32) < counts[:, None, None, None]
    return jnp.where(live, samples, 0.0)


def solution(mesh):
    placed = (
        P(None, None, "gx", "gy", None),
        P(("gx", "gy"), None, None),
        P(("gx", "gy"), None),
        P(("gx", "gy"), None, None, None),
        P(("gx", "gy")),
    )
    return jax.shard_map(
        local,
        mesh=mesh,
        in_specs=placed,
        out_specs=P(("gx", "gy"), None, None, None),
        check_vma=False,
    )
```

```python
import functools
import math

import jax
import jax.numpy as jnp
import numpy as np
from jax import lax
from jax.experimental import pallas as pl
from jax.experimental.pallas import tpu as pltpu
from jax.sharding import PartitionSpec as P

NX, NY, NZ = 512, 256, 256
GX, GY = 8, 16
DEVS = GX * GY
F32, BF16 = jnp.float32, jnp.bfloat16
VMEM_LIMIT = 48 * 2**20


def split_table(table):
    hi = table.astype(np.float32).astype(jnp.bfloat16)
    lo = (table - hi.astype(np.float64)).astype(np.float32).astype(jnp.bfloat16)
    return hi, lo


def angle(rows, columns, length):
    return (np.outer(rows, columns) % length) * (2.0 * math.pi / length)


def z_table():
    order = (np.arange(8)[:, None] + 8 * np.arange(32)[None, :]).reshape(-1)
    phase = angle(order, np.arange(NZ), NZ)
    scale = 1.0 / math.sqrt(NX * NY * NZ)
    return split_table(np.concatenate([np.cos(phase), np.sin(phase)], 1) * scale)


def x_table():
    phase = angle(np.arange(NX), np.arange(NX), NX)
    cos, sin = np.cos(phase), np.sin(phase)
    whole = np.zeros((2, NX, 2, NX))
    whole[0, :, 0], whole[1, :, 0] = cos, sin
    whole[0, :, 1], whole[1, :, 1] = -sin, cos
    whole = whole.reshape(2, 8, 64, 2, 64, 8).transpose(1, 0, 2, 5, 3, 4)
    return split_table(whole.reshape(1024, 1024))


def y_table():
    phase = angle(np.arange(NY), np.arange(NY), NY)
    cos, sin = np.cos(phase), np.sin(phase)
    whole = np.zeros((2, NY, 2, NY))
    whole[0, :, 0], whole[1, :, 0] = cos, sin
    whole[0, :, 1], whole[1, :, 1] = -sin, cos
    whole = whole.reshape(2, NY, 2, 32, 8).transpose(0, 1, 3, 2, 4)
    return split_table(whole.reshape(512, 512))


def halves(value):
    hi = value.astype(BF16)
    return hi, (value - hi.astype(F32)).astype(BF16)


def dot3(left, right, dims):
    def one(a, b):
        return lax.dot_general(a, b, (dims, ((), ())), preferred_element_type=F32)

    return one(left[0], right[0]) + (one(left[0], right[1]) + one(left[1], right[0]))


def z_kernel(near, far, hi, lo, out):
    def pair(yp, carry):
        rows, swapped = [], []
        for k in range(2):
            at = pl.ds(2 * yp + k, 64, stride=16)
            re, im = (jnp.concatenate([near[0, q, at, :], far[0, q, at, :]], 1) for q in range(2))
            rows += [re, im]
            swapped += [im, -re]
        data = jnp.concatenate(
            [jnp.concatenate(rows, 0), jnp.concatenate(swapped, 0)], 1
        )
        res = dot3((hi[...], lo[...]), halves(data), ((1,), (1,)))
        for k in range(2):
            out[:, 0, 2 * yp + k] = res[:, k * 128 : (k + 1) * 128].reshape(8, 32, 128)
        return carry

    lax.fori_loop(0, 8, pair, 0)


def z_transform(images):
    images = images.reshape(2, 2, 1024, 256)
    hi, lo = z_table()
    whole = pl.BlockSpec((256, 512), lambda c: (0, 0))
    return pl.pallas_call(
        z_kernel,
        out_shape=jax.ShapeDtypeStruct((8, 2, 16, 32, 128), F32),
        grid=(2,),
        in_specs=[
            pl.BlockSpec((1, 2, 1024, 128), lambda c: (c, 0, 0, 0)),
            pl.BlockSpec((1, 2, 1024, 128), lambda c: (c, 0, 0, 1)),
            whole,
            whole,
        ],
        out_specs=pl.BlockSpec((8, 1, 16, 32, 128), lambda c: (0, c, 0, 0, 0)),
        compiler_params=pltpu.CompilerParams(vmem_limit_bytes=VMEM_LIMIT),
        name="z_transform",
    )(images, images, jnp.asarray(hi), jnp.asarray(lo))


def x_kernel(data, hi, lo, out):
    rows = jnp.concatenate([data[a] for a in range(8)], 1)
    res = dot3(halves(rows), (hi[...], lo[...]), ((1,), (0,)))
    for u in range(8):
        out[u] = res[:, u * 128 : (u + 1) * 128]


def x_transform(data):
    hi, lo = x_table()
    whole = pl.BlockSpec((1024, 1024), lambda r: (0, 0))
    return pl.pallas_call(
        x_kernel,
        out_shape=jax.ShapeDtypeStruct((16, 512, 128), F32),
        grid=(4,),
        in_specs=[pl.BlockSpec((8, 256, 128), lambda r: (0, r, 0)), whole, whole],
        out_specs=pl.BlockSpec((8, 256, 128), lambda r: (r // 2, r % 2, 0)),
        compiler_params=pltpu.CompilerParams(vmem_limit_bytes=VMEM_LIMIT),
        name="x_transform",
    )(data, jnp.asarray(hi), jnp.asarray(lo))


def y_group(g, data, hi, lo, table):
    flat = data.reshape(2048, 128)
    lane = lax.broadcasted_iota(jnp.int32, (64, 128), 1)

    def four(p, carry):
        rows = []
        for k in range(4):
            turned = flat[pl.ds(4 * p + k, 256, stride=8), :].T
            rows.append(jnp.concatenate([turned[:64], turned[64:]], 1))
        res = dot3(halves(jnp.concatenate(rows, 0)), (hi[...], lo[...]), ((1,), (0,)))
        for k in range(4):
            bz = 8 * g + 4 * p + k
            for high in range(4):
                part = res[k * 64 : (k + 1) * 64, high * 128 : (high + 1) * 128]
                for low in range(8):
                    source = low * 16 + jnp.bitwise_and(lane, 15)
                    at = pl.multiple_of((bz * 32 + high * 8 + low) * 64, 64)
                    table[pl.ds(at, 64), :] = jnp.take_along_axis(part, source, axis=1)
        return carry

    lax.fori_loop(0, 2, four, 0)


def pick_group(rows, table, raw, out):
    def eight(t, carry):
        for s in range(8):
            for g in range(8):
                lanes = slice(g * 16, g * 16 + 16)
                row = rows[g * 256 + t * 8 + s]
                raw[pl.ds(t * 8 + s, 1), lanes] = table[pl.ds(row, 1), lanes]
        return carry

    lax.fori_loop(0, 32, eight, 0)
    for h in range(2):
        turned = raw[h * 128 : (h + 1) * 128, :].T
        for g in range(8):
            out[g, h] = turned[g * 16 : (g + 1) * 16]


def pick_kernel(data, rows, hi, lo, out, table, raw):
    g = pl.program_id(0)

    @pl.when(g < 4)
    def _():
        y_group(g, data, hi, lo, table)

    @pl.when(g >= 4)
    def _():
        pick_group(rows, table, raw, out)


def y_pick(data, rows):
    hi, lo = y_table()
    whole = pl.BlockSpec((512, 512), lambda g: (0, 0))
    late = lambda g: jnp.maximum(g - 4, 0)
    return pl.pallas_call(
        pick_kernel,
        out_shape=jax.ShapeDtypeStruct((128, 2, 16, 128), F32),
        grid=(20,),
        in_specs=[
            pl.BlockSpec((256, 8, 128), lambda g: (0, jnp.minimum(g, 3), 0)),
            pl.BlockSpec((2048,), lambda g: (late(g),), memory_space=pltpu.SMEM),
            whole,
            whole,
        ],
        out_specs=pl.BlockSpec((8, 2, 16, 128), lambda g: (late(g), 0, 0, 0)),
        scratch_shapes=[pltpu.VMEM((65536, 128), F32), pltpu.VMEM((256, 128), F32)],
        compiler_params=pltpu.CompilerParams(vmem_limit_bytes=VMEM_LIMIT),
        name="y_pick",
    )(data.reshape(256, 32, 128), rows, jnp.asarray(hi), jnp.asarray(lo))


def turn_kernel(weights, out):
    def one(n, carry):
        turned = weights[0, pl.ds(n, 128, stride=16), :].T
        for u in range(2):
            for v in range(8):
                at = (u * 8 + v) * 8
                out[0, n, pl.ds(u * 64 + v, 8, stride=8), :] = turned[at : at + 8]
        return carry

    lax.fori_loop(0, 16, one, 0)


def turn_weights(weights):
    return pl.pallas_call(
        turn_kernel,
        out_shape=jax.ShapeDtypeStruct((2, 16, 512, 128), F32),
        grid=(2, 4),
        in_specs=[pl.BlockSpec((1, 2048, 128), lambda h, e: (h, 0, e))],
        out_specs=pl.BlockSpec((1, 16, 128, 128), lambda h, e: (h, 0, e, 0)),
        compiler_params=pltpu.CompilerParams(vmem_limit_bytes=VMEM_LIMIT),
        name="turn_weights",
    )(weights.reshape(2, 2048, 512))


def sum_kernel(got, weights, out):
    def one(u, carry):
        sums = list(carry)
        for w in range(8):
            at = pl.multiple_of(u * 64 + w * 8, 8)
            factors = [weights[0, n, pl.ds(at, 8), :] for n in range(4)]
            for k in range(4):
                value = got[w, k // 2, u, 0, k % 2]
                for n in range(4):
                    sums[n * 4 + k] = sums[n * 4 + k] + factors[n] * value
        return tuple(sums)

    sums = lax.fori_loop(0, 8, one, (jnp.zeros((8, 128), F32),) * 16)
    rows = [jnp.sum(s, 0, keepdims=True) for s in sums]
    out[0, 0] = jnp.concatenate(rows, 0)


def interpolate(got, weights):
    return pl.pallas_call(
        sum_kernel,
        out_shape=jax.ShapeDtypeStruct((2, 4, 16, 128), F32),
        grid=(2, 4),
        in_specs=[
            pl.BlockSpec((8, 2, 8, 1, 2, 8, 128), lambda h, n: (0, 0, 0, h, 0, 0, 0)),
            pl.BlockSpec((1, 4, 512, 128), lambda h, n: (h, n, 0, 0)),
        ],
        out_specs=pl.BlockSpec((1, 1, 16, 128), lambda h, n: (h, n, 0, 0)),
        compiler_params=pltpu.CompilerParams(vmem_limit_bytes=VMEM_LIMIT),
        name="interpolate",
    )(got, weights)


def table_rows(send_lists, seg_slots):
    both = ("gx", "gy")
    lists = lax.all_to_all(send_lists[0], both, 0, 0, tiled=True).reshape(1, 512)
    hit = seg_slots.reshape(256, 1) == jnp.arange(512, dtype=jnp.int32)[None, :]
    ids = jnp.sum(jnp.where(hit, lists, 0), 1)
    rows = (ids & 31) * 2048 + ((ids >> 5) & 31) * 64 + (ids >> 10)
    sent = jnp.broadcast_to(rows[None, :], (DEVS, 256))
    return lax.all_to_all(sent, both, 0, 0, tiled=True).reshape(-1)


def local(coil_images, send_lists, seg_slots, weights, counts):
    rows = table_rows(send_lists, seg_slots)
    turned = turn_weights(weights)
    spectrum = z_transform(coil_images).reshape(8, 1024, 128)
    spectrum = lax.all_to_all(spectrum, "gx", 0, 0, tiled=True)
    spectrum = x_transform(spectrum)
    spectrum = lax.all_to_all(spectrum, "gy", 0, 0, tiled=True)
    sent = y_pick(spectrum, rows)
    got = lax.all_to_all(sent, ("gx", "gy"), 0, 0, tiled=True)
    sums = interpolate(got.reshape(8, 2, 8, 2, 2, 8, 128), turned)
    sums = sums.reshape(2, 16, 2, 2, 8, 16).sum(-1)
    samples = sums.transpose(0, 4, 2, 3, 1).reshape(16, 2, 2, 16)
    live = jnp.arange(16, dtype=jnp.int32) < counts[:, None, None, None]
    return jnp.where(live, samples, 0.0)


def solution(mesh):
    placed = (
        P(None, None, "gx", "gy", None),
        P(("gx", "gy"), None, None),
        P(("gx", "gy"), None),
        P(("gx", "gy"), None, None, None),
        P(("gx", "gy")),
    )
    return jax.shard_map(
        local,
        mesh=mesh,
        in_specs=placed,
        out_specs=P(("gx", "gy"), None, None, None),
        check_vma=False,
    )
```

```python
import functools
import math

import jax
import jax.numpy as jnp
import numpy as np
from jax import lax
from jax.experimental import pallas as pl
from jax.experimental.pallas import tpu as pltpu
from jax.sharding import PartitionSpec as P

NX, NY, NZ = 512, 256, 256
GX, GY = 8, 16
DEVS = GX * GY
F32, BF16 = jnp.float32, jnp.bfloat16
VMEM_LIMIT = 48 * 2**20


def split_table(table):
    hi = table.astype(np.float32).astype(jnp.bfloat16)
    lo = (table - hi.astype(np.float64)).astype(np.float32).astype(jnp.bfloat16)
    return hi, lo


def angle(rows, columns, length):
    return (np.outer(rows, columns) % length) * (2.0 * math.pi / length)


def z_table():
    bz = np.arange(32).reshape(4, 1, 8)
    order = (np.arange(8)[None, :, None] + 8 * bz).reshape(-1)
    phase = angle(order, np.arange(NZ), NZ)
    scale = 1.0 / math.sqrt(NX * NY * NZ)
    return split_table(np.concatenate([np.cos(phase), np.sin(phase)], 1) * scale)


def x_table():
    phase = angle(np.arange(NX), np.arange(NX), NX)
    cos, sin = np.cos(phase), np.sin(phase)
    whole = np.zeros((2, NX, 2, NX))
    whole[0, :, 0], whole[1, :, 0] = cos, sin
    whole[0, :, 1], whole[1, :, 1] = -sin, cos
    whole = whole.reshape(2, 8, 64, 2, 64, 8).transpose(1, 0, 2, 5, 3, 4)
    return split_table(whole.reshape(1024, 1024))


def y_table():
    phase = angle(np.arange(NY), np.arange(NY), NY)
    cos, sin = np.cos(phase), np.sin(phase)
    whole = np.zeros((2, NY, 2, NY))
    whole[0, :, 0], whole[1, :, 0] = cos, sin
    whole[0, :, 1], whole[1, :, 1] = -sin, cos
    whole = whole.reshape(2, NY, 2, 32, 8).transpose(0, 1, 3, 2, 4)
    return split_table(whole.reshape(512, 512))


def halves(value):
    hi = value.astype(BF16)
    return hi, (value - hi.astype(F32)).astype(BF16)


def dot3(left, right, dims):
    def one(a, b):
        return lax.dot_general(a, b, (dims, ((), ())), preferred_element_type=F32)

    return one(left[0], right[0]) + (one(left[0], right[1]) + one(left[1], right[0]))


def z_pair(yp, c, image, hi, lo, sent):
    rows, swapped = [], []
    for k in range(2):
        at = pl.ds(2 * yp + k, 64, stride=16)
        re, im = (
            jnp.concatenate([image[half, c, q, at, :] for half in range(2)], 1)
            for q in range(2)
        )
        rows += [re, im]
        swapped += [im, -re]
    data = jnp.concatenate([jnp.concatenate(rows, 0), jnp.concatenate(swapped, 0)], 1)
    res = dot3((hi[...], lo[...]), halves(data), ((1,), (1,)))
    for k in range(2):
        part = res[:, k * 128 : (k + 1) * 128].reshape(4, 8, 8, 128)
        sent[:, :, c, 2 * yp + k] = part


def grid_kernel(
    images, z_hi_in, z_lo_in, x_hi_in, x_lo_in, out,
    image, z_hi, z_lo, x_hi, x_lo, z_out, x_in, x_out,
    load_sem, self_sem, send1, recv1, send2, recv2,
):
    gx, gy = lax.axis_index("gx"), lax.axis_index("gy")
    loads = [
        pltpu.make_async_copy(src, dst, load_sem.at[i])
        for i, (src, dst) in enumerate(
            [(z_hi_in, z_hi), (z_lo_in, z_lo)]
            + [
                (images.at[c, q, :, pl.ds(half * 128, 128)], image.at[half, c, q])
                for c in range(2)
                for q in range(2)
                for half in range(2)
            ]
            + [(x_hi_in, x_hi), (x_lo_in, x_lo)]
        )
    ]
    for load in loads:
        load.start()

    barrier = pltpu.get_barrier_semaphore()
    for r in range(1, GX):
        pl.semaphore_signal(barrier, inc=1, device_id={"gx": (gx + r) % GX})
    for r in range(1, GY):
        pl.semaphore_signal(barrier, inc=1, device_id={"gy": (gy + r) % GY})
    pl.semaphore_wait(barrier, GX + GY - 2)

    def over_x(k, r):
        to = (gx + r) % GX
        return pltpu.make_async_remote_copy(
            src_ref=z_out.at[k, to],
            dst_ref=x_in.at[k, gx],
            send_sem=send1.at[k, r],
            recv_sem=recv1.at[k, r],
            device_id={"gx": to},
        )

    def over_y(k, r):
        to = (gy + r) % GY
        return pltpu.make_async_remote_copy(
            src_ref=x_out.at[k, to],
            dst_ref=out.at[k, gy],
            send_sem=send2.at[k, r],
            recv_sem=recv2.at[k, r],
            device_id={"gy": to},
        )

    def own_x(k):
        return pltpu.make_async_copy(z_out.at[k, gx], x_in.at[k, gx], self_sem.at[0, k])

    def own_y(k):
        return pltpu.make_async_copy(x_out.at[k, gy], out.at[k, gy], self_sem.at[1, k])

    for load in loads[:2]:
        load.wait()
    for c in range(2):
        for load in loads[2 + 4 * c : 6 + 4 * c]:
            load.wait()

        def pair(yp, carry):
            z_pair(yp, c, image, z_hi, z_lo, z_out)
            return carry

        lax.fori_loop(0, 8, pair, 0)
    for load in loads[10:]:
        load.wait()

    def send_x(k, carry):
        for r in range(1, GX):
            over_x(k, r).start()
        own_x(k).start()
        return carry

    lax.fori_loop(0, 4, send_x, 0)

    def chunk(k, carry):
        own_x(k).wait()
        for r in range(1, GX):
            over_x(k, r).wait_recv()
        rows = jnp.concatenate(
            [x_in[k, a].reshape(256, 128) for a in range(8)], 1
        )
        res = dot3(halves(rows), (x_hi[...], x_lo[...]), ((1,), (0,)))
        for c in range(2):
            for u in range(8):
                x_out[k, c * 8 + u] = res[
                    c * 128 : (c + 1) * 128, u * 128 : (u + 1) * 128
                ].reshape(16, 8, 128)
        for r in range(1, GY):
            over_y(k, r).start()
        own_y(k).start()
        return carry

    lax.fori_loop(0, 4, chunk, 0)

    def finish(k, carry):
        own_y(k).wait()
        for r in range(1, GX):
            over_x(k, r).wait_send()
        for r in range(1, GY):
            over_y(k, r).wait()
        return carry

    lax.fori_loop(0, 4, finish, 0)


def grid_values(images):
    tables = [jnp.asarray(t) for t in z_table() + x_table()]
    anywhere = pl.BlockSpec(memory_space=pl.ANY)
    sems = pltpu.SemaphoreType.DMA
    return pl.pallas_call(
        grid_kernel,
        out_shape=jax.ShapeDtypeStruct((4, 16, 16, 8, 128), F32),
        in_specs=[anywhere] * 5,
        out_specs=anywhere,
        scratch_shapes=[
            pltpu.VMEM((2, 2, 2, 1024, 128), F32),
            pltpu.VMEM((256, 512), BF16),
            pltpu.VMEM((256, 512), BF16),
            pltpu.VMEM((1024, 1024), BF16),
            pltpu.VMEM((1024, 1024), BF16),
            pltpu.VMEM((4, 8, 2, 16, 8, 128), F32),
            pltpu.VMEM((4, 8, 2, 16, 8, 128), F32),
            pltpu.VMEM((4, 16, 16, 8, 128), F32),
            sems((12,)),
            sems((2, 4)),
            sems((4, GX)),
            sems((4, GX)),
            sems((4, GY)),
            sems((4, GY)),
        ],
        compiler_params=pltpu.CompilerParams(
            vmem_limit_bytes=VMEM_LIMIT, collective_id=0, has_side_effects=True
        ),
        name="grid_values",
    )(images.reshape(2, 2, 1024, 256), *tables)


def y_group(g, data, hi, lo, table):
    lane = lax.broadcasted_iota(jnp.int32, (64, 128), 1)

    def four(p, carry):
        rows = []
        for k in range(4):
            turned = data[pl.ds(4 * p + k, 256, stride=8), :].T
            rows.append(jnp.concatenate([turned[:64], turned[64:]], 1))
        res = dot3(halves(jnp.concatenate(rows, 0)), (hi[...], lo[...]), ((1,), (0,)))
        for k in range(4):
            bz = 8 * g + 4 * p + k
            for high in range(4):
                part = res[k * 64 : (k + 1) * 64, high * 128 : (high + 1) * 128]
                for low in range(8):
                    source = low * 16 + jnp.bitwise_and(lane, 15)
                    at = pl.multiple_of((bz * 32 + high * 8 + low) * 64, 64)
                    table[pl.ds(at, 64), :] = jnp.take_along_axis(part, source, axis=1)
        return carry

    lax.fori_loop(0, 2, four, 0)


def pick_group(rows, table, raw, out):
    def eight(t, carry):
        for s in range(8):
            for g in range(8):
                lanes = slice(g * 16, g * 16 + 16)
                row = rows[g * 256 + t * 8 + s]
                raw[pl.ds(t * 8 + s, 1), lanes] = table[pl.ds(row, 1), lanes]
        return carry

    lax.fori_loop(0, 32, eight, 0)
    for h in range(2):
        turned = raw[h * 128 : (h + 1) * 128, :].T
        for g in range(8):
            out[g, h] = turned[g * 16 : (g + 1) * 16]


def pick_kernel(data, rows, hi, lo, out, table, raw):
    g = pl.program_id(0)

    @pl.when(g < 4)
    def _():
        y_group(g, data, hi, lo, table)

    @pl.when(g >= 4)
    def _():
        pick_group(rows, table, raw, out)


def y_pick(data, rows):
    hi, lo = y_table()
    whole = pl.BlockSpec((512, 512), lambda g: (0, 0))
    late = lambda g: jnp.maximum(g - 4, 0)
    return pl.pallas_call(
        pick_kernel,
        out_shape=jax.ShapeDtypeStruct((128, 2, 16, 128), F32),
        grid=(20,),
        in_specs=[
            pl.BlockSpec((2048, 128), lambda g: (jnp.minimum(g, 3), 0)),
            pl.BlockSpec((2048,), lambda g: (late(g),), memory_space=pltpu.SMEM),
            whole,
            whole,
        ],
        out_specs=pl.BlockSpec((8, 2, 16, 128), lambda g: (late(g), 0, 0, 0)),
        scratch_shapes=[pltpu.VMEM((65536, 128), F32), pltpu.VMEM((256, 128), F32)],
        compiler_params=pltpu.CompilerParams(vmem_limit_bytes=VMEM_LIMIT),
        name="y_pick",
    )(data.reshape(8192, 128), rows, jnp.asarray(hi), jnp.asarray(lo))


def turn_kernel(weights, out):
    def one(n, carry):
        turned = weights[0, pl.ds(n, 128, stride=16), :].T
        for u in range(2):
            for v in range(8):
                at = (u * 8 + v) * 8
                out[0, n, pl.ds(u * 64 + v, 8, stride=8), :] = turned[at : at + 8]
        return carry

    lax.fori_loop(0, 16, one, 0)


def turn_weights(weights):
    return pl.pallas_call(
        turn_kernel,
        out_shape=jax.ShapeDtypeStruct((2, 16, 512, 128), F32),
        grid=(2, 4),
        in_specs=[pl.BlockSpec((1, 2048, 128), lambda h, e: (h, 0, e))],
        out_specs=pl.BlockSpec((1, 16, 128, 128), lambda h, e: (h, 0, e, 0)),
        compiler_params=pltpu.CompilerParams(vmem_limit_bytes=VMEM_LIMIT),
        name="turn_weights",
    )(weights.reshape(2, 2048, 512))


def sum_kernel(got, weights, out):
    def one(u, carry):
        sums = list(carry)
        for w in range(8):
            at = pl.multiple_of(u * 64 + w * 8, 8)
            factors = [weights[0, n, pl.ds(at, 8), :] for n in range(4)]
            for k in range(4):
                value = got[w, k // 2, u, 0, k % 2]
                for n in range(4):
                    sums[n * 4 + k] = sums[n * 4 + k] + factors[n] * value
        return tuple(sums)

    sums = lax.fori_loop(0, 8, one, (jnp.zeros((8, 128), F32),) * 16)
    rows = [jnp.sum(s, 0, keepdims=True) for s in sums]
    out[0, 0] = jnp.concatenate(rows, 0)


def interpolate(got, weights):
    return pl.pallas_call(
        sum_kernel,
        out_shape=jax.ShapeDtypeStruct((2, 4, 16, 128), F32),
        grid=(2, 4),
        in_specs=[
            pl.BlockSpec((8, 2, 8, 1, 2, 8, 128), lambda h, n: (0, 0, 0, h, 0, 0, 0)),
            pl.BlockSpec((1, 4, 512, 128), lambda h, n: (h, n, 0, 0)),
        ],
        out_specs=pl.BlockSpec((1, 1, 16, 128), lambda h, n: (h, n, 0, 0)),
        compiler_params=pltpu.CompilerParams(vmem_limit_bytes=VMEM_LIMIT),
        name="interpolate",
    )(got, weights)


def table_rows(send_lists, seg_slots):
    both = ("gx", "gy")
    lists = lax.all_to_all(send_lists[0], both, 0, 0, tiled=True).reshape(1, 512)
    hit = seg_slots.reshape(256, 1) == jnp.arange(512, dtype=jnp.int32)[None, :]
    ids = jnp.sum(jnp.where(hit, lists, 0), 1)
    rows = (ids & 31) * 2048 + ((ids >> 5) & 31) * 64 + (ids >> 10)
    sent = jnp.broadcast_to(rows[None, :], (DEVS, 256))
    return lax.all_to_all(sent, both, 0, 0, tiled=True).reshape(-1)


def local(coil_images, send_lists, seg_slots, weights, counts):
    rows = table_rows(send_lists, seg_slots)
    turned = turn_weights(weights)
    spectrum = grid_values(coil_images)
    sent = y_pick(spectrum, rows)
    got = lax.all_to_all(sent, ("gx", "gy"), 0, 0, tiled=True)
    sums = interpolate(got.reshape(8, 2, 8, 2, 2, 8, 128), turned)
    sums = sums.reshape(2, 16, 2, 2, 8, 16).sum(-1)
    samples = sums.transpose(0, 4, 2, 3, 1).reshape(16, 2, 2, 16)
    live = jnp.arange(16, dtype=jnp.int32) < counts[:, None, None, None]
    return jnp.where(live, samples, 0.0)


def solution(mesh):
    placed = (
        P(None, None, "gx", "gy", None),
        P(("gx", "gy"), None, None),
        P(("gx", "gy"), None),
        P(("gx", "gy"), None, None, None),
        P(("gx", "gy")),
    )
    return jax.shard_map(
        local,
        mesh=mesh,
        in_specs=placed,
        out_specs=P(("gx", "gy"), None, None, None),
        check_vma=False,
    )
```

```python
import functools
import math

import jax
import jax.numpy as jnp
import numpy as np
from jax import lax
from jax.experimental import pallas as pl
from jax.experimental.pallas import tpu as pltpu
from jax.sharding import PartitionSpec as P

NX, NY, NZ = 512, 256, 256
GX, GY = 8, 16
DEVS = GX * GY
F32, BF16 = jnp.float32, jnp.bfloat16
VMEM_LIMIT = 48 * 2**20


def split_table(table):
    hi = table.astype(np.float32).astype(jnp.bfloat16)
    lo = (table - hi.astype(np.float64)).astype(np.float32).astype(jnp.bfloat16)
    return hi, lo


def angle(rows, columns, length):
    return (np.outer(rows, columns) % length) * (2.0 * math.pi / length)


def z_table():
    bz = np.arange(32).reshape(4, 1, 8)
    order = (np.arange(8)[None, :, None] + 8 * bz).reshape(-1)
    phase = angle(order, np.arange(NZ), NZ)
    scale = 1.0 / math.sqrt(NX * NY * NZ)
    return split_table(np.concatenate([np.cos(phase), np.sin(phase)], 1) * scale)


def x_table():
    phase = angle(np.arange(NX), np.arange(NX), NX)
    cos, sin = np.cos(phase), np.sin(phase)
    whole = np.zeros((2, NX, 2, NX))
    whole[0, :, 0], whole[1, :, 0] = cos, sin
    whole[0, :, 1], whole[1, :, 1] = -sin, cos
    whole = whole.reshape(2, 8, 64, 2, 64, 8).transpose(1, 0, 2, 5, 3, 4)
    return split_table(whole.reshape(1024, 1024))


def y_table():
    phase = angle(np.arange(NY), np.arange(NY), NY)
    cos, sin = np.cos(phase), np.sin(phase)
    whole = np.zeros((2, NY, 2, NY))
    whole[0, :, 0], whole[1, :, 0] = cos, sin
    whole[0, :, 1], whole[1, :, 1] = -sin, cos
    whole = whole.reshape(2, NY, 2, 32, 8).transpose(0, 1, 3, 2, 4)
    return split_table(whole.reshape(512, 512))


def halves(value):
    hi = value.astype(BF16)
    return hi, (value - hi.astype(F32)).astype(BF16)


def dot3(left, right, dims):
    def one(a, b):
        return lax.dot_general(a, b, (dims, ((), ())), preferred_element_type=F32)

    return one(left[0], right[0]) + (one(left[0], right[1]) + one(left[1], right[0]))


def z_pair(yp, c, image, hi, lo, sent):
    rows, swapped = [], []
    for k in range(2):
        at = pl.ds(2 * yp + k, 64, stride=16)
        re, im = (
            jnp.concatenate([image[half, c, q, at, :] for half in range(2)], 1)
            for q in range(2)
        )
        rows += [re, im]
        swapped += [im, -re]
    data = jnp.concatenate([jnp.concatenate(rows, 0), jnp.concatenate(swapped, 0)], 1)
    res = dot3((hi[...], lo[...]), halves(data), ((1,), (1,)))
    for k in range(2):
        part = res[:, k * 128 : (k + 1) * 128].reshape(4, 8, 8, 128)
        sent[:, :, c, 2 * yp + k] = part


def hops(pairs, axis, size, sems):
    me = lax.axis_index(axis)
    src, dst = pairs
    made = []
    for r in range(1, size):
        to = (me + r) % size
        made.append(
            pltpu.make_async_remote_copy(
                src_ref=src(to),
                dst_ref=dst,
                send_sem=sems.at[0, r],
                recv_sem=sems.at[1, r],
                device_id={axis: to},
            )
        )
    return made


def own_rows(listed, slots, mine, gy):
    lists = listed[...].reshape(128, 128).astype(F32)
    lists = pltpu.roll(lists, 64 - 4 * gy, 1)
    row = lax.broadcasted_iota(jnp.int32, (128, 128), 0)
    first = row % 8 * 64 + row // 8 * 4
    for h in range(2):
        wanted = slots[h : h + 1, :]
        total = jnp.zeros((1, 128), F32)
        for k in range(4):
            column = jnp.broadcast_to(lists[:, 64 + k : 65 + k], (128, 128))
            hit = first + k == wanted
            total += jnp.sum(jnp.where(hit, column, 0.0), 0, keepdims=True)
        ids = total.astype(jnp.int32)
        low, high = jnp.bitwise_and(ids, 31), jnp.right_shift(ids, 5)
        rows = low * 2048 + jnp.bitwise_and(high, 31) * 64 + jnp.right_shift(high, 5)
        mine[h : h + 1, :] = rows


def turn_unit(block, turned):
    def one(n, carry):
        part = block[pl.ds(n, 128, stride=16), :].T
        for u in range(2):
            for v in range(8):
                at = (u * 8 + v) * 8
                turned[n, pl.ds(u * 64 + v, 8, stride=8), :] = part[at : at + 8]
        return carry

    lax.fori_loop(0, 16, one, 0)


def grid_kernel(
    images, z_hi_in, z_lo_in, x_hi_in, x_lo_in, lists, slots, weights,
    out, rows_out, turned_out,
    image, z_hi, z_lo, x_hi, x_lo, z_out, x_in, x_out,
    near, near8, listed, mine, mine8, block, turned,
    load_sem, self_sem, send1, recv1, send2, recv2,
    small1, small2, small3, small4, block_sem, turned_sem,
):
    gx, gy = lax.axis_index("gx"), lax.axis_index("gy")
    loads = [
        pltpu.make_async_copy(src, dst, load_sem.at[i])
        for i, (src, dst) in enumerate(
            [(z_hi_in, z_hi), (z_lo_in, z_lo)]
            + [
                (images.at[c, q, :, pl.ds(half * 128, 128)], image.at[half, c, q])
                for c in range(2)
                for q in range(2)
                for half in range(2)
            ]
            + [(x_hi_in, x_hi), (x_lo_in, x_lo)]
        )
    ]
    for load in loads:
        load.start()

    barrier = pltpu.get_barrier_semaphore()
    for r in range(1, GX):
        pl.semaphore_signal(barrier, inc=1, device_id={"gx": (gx + r) % GX})
    for r in range(1, GY):
        pl.semaphore_signal(barrier, inc=1, device_id={"gy": (gy + r) % GY})
    pl.semaphore_wait(barrier, GX + GY - 2)

    def over_x(k, r):
        to = (gx + r) % GX
        return pltpu.make_async_remote_copy(
            src_ref=z_out.at[k, to],
            dst_ref=x_in.at[k, gx],
            send_sem=send1.at[k, r],
            recv_sem=recv1.at[k, r],
            device_id={"gx": to},
        )

    def over_y(k, r):
        to = (gy + r) % GY
        return pltpu.make_async_remote_copy(
            src_ref=x_out.at[k, to],
            dst_ref=out.at[k, gy],
            send_sem=send2.at[k, r],
            recv_sem=recv2.at[k, r],
            device_id={"gy": to},
        )

    def own_x(k):
        return pltpu.make_async_copy(z_out.at[k, gx], x_in.at[k, gx], self_sem.at[0, k])

    def own_y(k):
        return pltpu.make_async_copy(x_out.at[k, gy], out.at[k, gy], self_sem.at[1, k])

    hop1 = hops((lambda to: lists.at[to], near.at[gx]), "gx", GX, small1)
    hop2 = hops((lambda to: near8, listed.at[gy]), "gy", GY, small2)
    hop3 = hops((lambda to: mine, mine8.at[gx]), "gx", GX, small3)
    hop4 = hops((lambda to: mine8, rows_out.at[gy]), "gy", GY, small4)
    own4 = pltpu.make_async_copy(mine8, rows_out.at[gy], self_sem.at[2, 0])

    def fetch(j, slot):
        src = weights.at[j // 4, :, pl.ds(j % 4 * 128, 128)]
        return pltpu.make_async_copy(src, block.at[slot], block_sem.at[slot])

    def put(j, slot):
        dst = turned_out.at[j // 4, :, pl.ds(j % 4 * 128, 128), :]
        return pltpu.make_async_copy(turned.at[slot], dst, turned_sem.at[slot])

    for hop in hop1:
        hop.start()
    for slot in range(2):
        fetch(slot, slot).start()

    for load in loads[:2]:
        load.wait()
    for c in range(2):
        for load in loads[2 + 4 * c : 6 + 4 * c]:
            load.wait()

        def pair(yp, carry):
            z_pair(yp, c, image, z_hi, z_lo, z_out)
            return carry

        lax.fori_loop(0, 8, pair, 0)
    for load in loads[10:]:
        load.wait()

    def send_x(k, carry):
        for r in range(1, GX):
            over_x(k, r).start()
        own_x(k).start()
        return carry

    lax.fori_loop(0, 4, send_x, 0)

    near[gx] = lists[gx]
    for hop in hop1:
        hop.wait()
    for a in range(GX):
        near8[a : a + 1, :] = near[a]
    for hop in hop2:
        hop.start()
    listed[gy] = near8[...]

    def chunk(k, carry):
        for slot in range(2):
            fetch(2 * k + slot, slot).wait()

            @pl.when(k > 0)
            def _():
                put(2 * k + slot - 2, slot).wait()

            turn_unit(block.at[slot], turned.at[slot])
            put(2 * k + slot, slot).start()

            @pl.when(k < 3)
            def _():
                fetch(2 * k + slot + 2, slot).start()

        own_x(k).wait()
        for r in range(1, GX):
            over_x(k, r).wait_recv()
        rows = jnp.concatenate(
            [x_in[k, a].reshape(256, 128) for a in range(8)], 1
        )
        res = dot3(halves(rows), (x_hi[...], x_lo[...]), ((1,), (0,)))
        for c in range(2):
            for u in range(8):
                x_out[k, c * 8 + u] = res[
                    c * 128 : (c + 1) * 128, u * 128 : (u + 1) * 128
                ].reshape(16, 8, 128)
        for r in range(1, GY):
            over_y(k, r).start()
        own_y(k).start()

        @pl.when(k == 0)
        def _():
            for hop in hop2:
                hop.wait()
            own_rows(listed, slots, mine, gy)
            for hop in hop3:
                hop.start()
            mine8[gx] = mine[...]

        @pl.when(k == 1)
        def _():
            for hop in hop3:
                hop.wait()
            for hop in hop4:
                hop.start()
            own4.start()

        return carry

    lax.fori_loop(0, 4, chunk, 0)
    for hop in hop4:
        hop.wait()
    own4.wait()
    for slot in range(2):
        put(6 + slot, slot).wait()

    def finish(k, carry):
        own_y(k).wait()
        for r in range(1, GX):
            over_x(k, r).wait_send()
        for r in range(1, GY):
            over_y(k, r).wait()
        return carry

    lax.fori_loop(0, 4, finish, 0)


def grid_values(images, lists, slots, weights):
    tables = [jnp.asarray(t) for t in z_table() + x_table()]
    anywhere = pl.BlockSpec(memory_space=pl.ANY)
    inside = pl.BlockSpec(memory_space=pltpu.VMEM)
    dma = pltpu.SemaphoreType.DMA
    i32 = jnp.int32
    return pl.pallas_call(
        grid_kernel,
        out_shape=(
            jax.ShapeDtypeStruct((4, 16, 16, 8, 128), F32),
            jax.ShapeDtypeStruct((GY, GX, 2, 128), i32),
            jax.ShapeDtypeStruct((2, 16, 512, 128), F32),
        ),
        in_specs=[anywhere] * 5 + [inside] * 2 + [anywhere],
        out_specs=(anywhere,) * 3,
        scratch_shapes=[
            pltpu.VMEM((2, 2, 2, 1024, 128), F32),
            pltpu.VMEM((256, 512), BF16),
            pltpu.VMEM((256, 512), BF16),
            pltpu.VMEM((1024, 1024), BF16),
            pltpu.VMEM((1024, 1024), BF16),
            pltpu.VMEM((4, 8, 2, 16, 8, 128), F32),
            pltpu.VMEM((4, 8, 2, 16, 8, 128), F32),
            pltpu.VMEM((4, 16, 16, 8, 128), F32),
            pltpu.VMEM((GX, 1, 128), i32),
            pltpu.VMEM((GX, 128), i32),
            pltpu.VMEM((GY, GX, 128), i32),
            pltpu.VMEM((2, 128), i32),
            pltpu.VMEM((GX, 2, 128), i32),
            pltpu.VMEM((2, 2048, 128), F32),
            pltpu.VMEM((2, 16, 128, 128), F32),
            dma((12,)),
            dma((3, 4)),
            dma((4, GX)),
            dma((4, GX)),
            dma((4, GY)),
            dma((4, GY)),
            dma((2, GX)),
            dma((2, GY)),
            dma((2, GX)),
            dma((2, GY)),
            dma((2,)),
            dma((2,)),
        ],
        compiler_params=pltpu.CompilerParams(
            vmem_limit_bytes=VMEM_LIMIT, collective_id=0, has_side_effects=True
        ),
        name="grid_values",
    )(images, *tables, lists, slots, weights)


def y_group(g, data, hi, lo, table):
    lane = lax.broadcasted_iota(jnp.int32, (64, 128), 1)

    def four(p, carry):
        rows = []
        for k in range(4):
            turned = data[pl.ds(4 * p + k, 256, stride=8), :].T
            rows.append(jnp.concatenate([turned[:64], turned[64:]], 1))
        res = dot3(halves(jnp.concatenate(rows, 0)), (hi[...], lo[...]), ((1,), (0,)))
        for k in range(4):
            bz = 8 * g + 4 * p + k
            for high in range(4):
                part = res[k * 64 : (k + 1) * 64, high * 128 : (high + 1) * 128]
                for low in range(8):
                    source = low * 16 + jnp.bitwise_and(lane, 15)
                    at = pl.multiple_of((bz * 32 + high * 8 + low) * 64, 64)
                    table[pl.ds(at, 64), :] = jnp.take_along_axis(part, source, axis=1)
        return carry

    lax.fori_loop(0, 2, four, 0)


def pick_group(bases, rows, table, raw, out):
    def eight(t, carry):
        for s in range(8):
            for g in range(8):
                lanes = slice(g * 16, g * 16 + 16)
                row = rows[bases[g] + t * 8 + s]
                raw[pl.ds(t * 8 + s, 1), lanes] = table[pl.ds(row, 1), lanes]
        return carry

    lax.fori_loop(0, 32, eight, 0)
    for h in range(2):
        turned = raw[h * 128 : (h + 1) * 128, :].T
        for g in range(8):
            out[g, h] = turned[g * 16 : (g + 1) * 16]


def pick_kernel(data_in, rows, hi, lo, out, data, table, raw, sent, load_sem, self_sem, send, recv):
    gx, gy = lax.axis_index("gx"), lax.axis_index("gy")
    me = gx * GY + gy
    loads = [
        pltpu.make_async_copy(data_in.at[k], data.at[k], load_sem.at[k]) for k in range(4)
    ]
    for load in loads:
        load.start()
    barrier = pltpu.get_barrier_semaphore()

    def greet(o, carry):
        to = (me + o) % DEVS
        pl.semaphore_signal(barrier, inc=1, device_id={"gx": to // GY, "gy": to % GY})
        return carry

    lax.fori_loop(1, DEVS, greet, 0)

    for k in range(4):
        loads[k].wait()
        y_group(k, data.at[k], hi, lo, table)

    pl.semaphore_wait(barrier, DEVS - 1)

    def copy(i, g):
        return pltpu.make_async_remote_copy(
            src_ref=sent.at[i, g],
            dst_ref=out.at[me],
            send_sem=send.at[i, g],
            recv_sem=recv.at[i, g],
            device_id={"gx": (gx + g) % GX, "gy": (gy + i) % GY},
        )

    own = pltpu.make_async_copy(sent.at[0, 0], out.at[me], self_sem)

    def group(i, carry):
        to = (gy + i) % GY
        bases = [to * 2048 + (gx + g) % GX * 256 for g in range(8)]
        pick_group(bases, rows, table, raw, sent.at[i])

        @pl.when(i == 0)
        def _():
            own.start()

        @pl.when(i > 0)
        def _():
            copy(i, 0).start()

        for g in range(1, 8):
            copy(i, g).start()
        return carry

    lax.fori_loop(0, 16, group, 0)
    own.wait()

    def finish(i, carry):
        @pl.when(i > 0)
        def _():
            copy(i, 0).wait()

        for g in range(1, 8):
            copy(i, g).wait()
        return carry

    lax.fori_loop(0, 16, finish, 0)


def y_pick(data, rows):
    hi, lo = y_table()
    anywhere = pl.BlockSpec(memory_space=pl.ANY)
    inside = pl.BlockSpec(memory_space=pltpu.VMEM)
    dma = pltpu.SemaphoreType.DMA
    return pl.pallas_call(
        pick_kernel,
        out_shape=jax.ShapeDtypeStruct((128, 2, 16, 128), F32),
        in_specs=[anywhere, pl.BlockSpec(memory_space=pltpu.SMEM), inside, inside],
        out_specs=anywhere,
        scratch_shapes=[
            pltpu.VMEM((4, 2048, 128), F32),
            pltpu.VMEM((65536, 128), F32),
            pltpu.VMEM((256, 128), F32),
            pltpu.VMEM((16, 8, 2, 16, 128), F32),
            dma((4,)),
            dma,
            dma((16, 8)),
            dma((16, 8)),
        ],
        compiler_params=pltpu.CompilerParams(
            vmem_limit_bytes=VMEM_LIMIT, collective_id=1, has_side_effects=True
        ),
        name="y_pick",
    )(data, rows, jnp.asarray(hi), jnp.asarray(lo))


def sum_kernel(got, weights, out):
    def one(u, carry):
        sums = list(carry)
        for w in range(8):
            at = pl.multiple_of(u * 64 + w * 8, 8)
            factors = [weights[0, n, pl.ds(at, 8), :] for n in range(4)]
            for k in range(4):
                value = got[w, k // 2, u, 0, k % 2]
                for n in range(4):
                    sums[n * 4 + k] = sums[n * 4 + k] + factors[n] * value
        return tuple(sums)

    sums = lax.fori_loop(0, 8, one, (jnp.zeros((8, 128), F32),) * 16)
    rows = [jnp.sum(s, 0, keepdims=True) for s in sums]
    out[0, 0] = jnp.concatenate(rows, 0)


def interpolate(got, weights):
    return pl.pallas_call(
        sum_kernel,
        out_shape=jax.ShapeDtypeStruct((2, 4, 16, 128), F32),
        grid=(2, 4),
        in_specs=[
            pl.BlockSpec((8, 2, 8, 1, 2, 8, 128), lambda h, n: (0, 0, 0, h, 0, 0, 0)),
            pl.BlockSpec((1, 4, 512, 128), lambda h, n: (h, n, 0, 0)),
        ],
        out_specs=pl.BlockSpec((1, 1, 16, 128), lambda h, n: (h, n, 0, 0)),
        compiler_params=pltpu.CompilerParams(vmem_limit_bytes=VMEM_LIMIT),
        name="interpolate",
    )(got, weights)


def local(coil_images, send_lists, seg_slots, weights, counts):
    lists = jnp.pad(send_lists.reshape(GX, 1, 64), ((0, 0), (0, 0), (0, 64)))
    values, rows, turned = grid_values(
        coil_images.reshape(2, 2, 1024, 256),
        lists,
        seg_slots.reshape(2, 128),
        weights.reshape(2, 2048, 512),
    )
    got = y_pick(values.reshape(4, 2048, 128), rows.reshape(-1))
    sums = interpolate(got.reshape(8, 2, 8, 2, 2, 8, 128), turned)
    sums = sums.reshape(2, 16, 2, 2, 8, 16).sum(-1)
    samples = sums.transpose(0, 4, 2, 3, 1).reshape(16, 2, 2, 16)
    live = jnp.arange(16, dtype=jnp.int32) < counts[:, None, None, None]
    return jnp.where(live, samples, 0.0)


def solution(mesh):
    placed = (
        P(None, None, "gx", "gy", None),
        P(("gx", "gy"), None, None),
        P(("gx", "gy"), None),
        P(("gx", "gy"), None, None, None),
        P(("gx", "gy")),
    )
    return jax.shard_map(
        local,
        mesh=mesh,
        in_specs=placed,
        out_specs=P(("gx", "gy"), None, None, None),
        check_vma=False,
    )
```

```python
import functools
import math

import jax
import jax.numpy as jnp
import numpy as np
from jax import lax
from jax.experimental import pallas as pl
from jax.experimental.pallas import tpu as pltpu
from jax.sharding import PartitionSpec as P

NX, NY, NZ = 512, 256, 256
GX, GY = 8, 16
DEVS = GX * GY
F32, BF16 = jnp.float32, jnp.bfloat16
WIDE_VMEM = 62 * 2**20


def split_table(table):
    hi = table.astype(np.float32).astype(jnp.bfloat16)
    lo = (table - hi.astype(np.float64)).astype(np.float32).astype(jnp.bfloat16)
    return hi, lo


def angle(rows, columns, length):
    return (np.outer(rows, columns) % length) * (2.0 * math.pi / length)


def z_table():
    bz = np.arange(32).reshape(4, 1, 8)
    order = (np.arange(8)[None, :, None] + 8 * bz).reshape(-1)
    phase = angle(order, np.arange(NZ), NZ)
    scale = 1.0 / math.sqrt(NX * NY * NZ)
    return split_table(np.concatenate([np.cos(phase), np.sin(phase)], 1) * scale)


def x_table():
    phase = angle(np.arange(NX), np.arange(NX), NX)
    cos, sin = np.cos(phase), np.sin(phase)
    whole = np.zeros((2, NX, 2, NX))
    whole[0, :, 0], whole[1, :, 0] = cos, sin
    whole[0, :, 1], whole[1, :, 1] = -sin, cos
    whole = whole.reshape(2, 8, 64, 2, 64, 8).transpose(1, 0, 2, 5, 3, 4)
    return split_table(whole.reshape(1024, 1024))


def y_table():
    phase = angle(np.arange(NY), np.arange(NY), NY)
    cos, sin = np.cos(phase), np.sin(phase)
    whole = np.zeros((2, NY, 2, NY))
    whole[0, :, 0], whole[1, :, 0] = cos, sin
    whole[0, :, 1], whole[1, :, 1] = -sin, cos
    whole = whole.reshape(2, NY, 2, 32, 8).transpose(0, 1, 3, 2, 4)
    return split_table(whole.reshape(512, 512))


def halves(value):
    hi = value.astype(BF16)
    return hi, (value - hi.astype(F32)).astype(BF16)


def dot3(left, right, dims):
    def one(a, b):
        return lax.dot_general(a, b, (dims, ((), ())), preferred_element_type=F32)

    return one(left[0], right[0]) + (one(left[0], right[1]) + one(left[1], right[0]))


def z_pair(yp, c, image, hi, lo, sent):
    rows, swapped = [], []
    for k in range(2):
        at = pl.ds(2 * yp + k, 64, stride=16)
        re, im = (
            jnp.concatenate([image[half, c, q, at, :] for half in range(2)], 1)
            for q in range(2)
        )
        rows += [re, im]
        swapped += [im, -re]
    data = jnp.concatenate([jnp.concatenate(rows, 0), jnp.concatenate(swapped, 0)], 1)
    res = dot3((hi[...], lo[...]), halves(data), ((1,), (1,)))
    for k in range(2):
        part = res[:, k * 128 : (k + 1) * 128].reshape(4, 8, 8, 128)
        y = 2 * yp + k
        for b in range(4):
            sent[y // 8 * 4 + b, :, c, y % 8] = part[b]


def hops(pairs, axis, size, sems):
    me = lax.axis_index(axis)
    src, dst = pairs
    made = []
    for r in range(1, size):
        to = (me + r) % size
        made.append(
            pltpu.make_async_remote_copy(
                src_ref=src(to),
                dst_ref=dst,
                send_sem=sems.at[0, r],
                recv_sem=sems.at[1, r],
                device_id={axis: to},
            )
        )
    return made


def own_rows(listed, slots, mine, gy):
    lists = listed[...].reshape(128, 128).astype(F32)
    lists = pltpu.roll(lists, (128 - gy) % 128, 1)
    row = lax.broadcasted_iota(jnp.int32, (128, 128), 0)
    first = row % 8 * 64 + row // 8 * 4
    for h in range(2):
        wanted = slots[h : h + 1, :]
        total = jnp.zeros((1, 128), F32)
        for k in range(4):
            column = jnp.broadcast_to(lists[:, 16 * k : 16 * k + 1], (128, 128))
            hit = first + k == wanted
            total += jnp.sum(jnp.where(hit, column, 0.0), 0, keepdims=True)
        ids = total.astype(jnp.int32)
        low, high = jnp.bitwise_and(ids, 31), jnp.right_shift(ids, 5)
        rows = low * 2048 + jnp.bitwise_and(high, 31) * 64 + jnp.right_shift(high, 5)
        mine[h : h + 1, :] = rows


def turn_unit(block, turned):
    def one(n, carry):
        part = block[pl.ds(n, 128, stride=16), :].T
        for u in range(2):
            for v in range(8):
                at = (u * 8 + v) * 8
                turned[n, pl.ds(u * 64 + v, 8, stride=8), :] = part[at : at + 8]
        return carry

    lax.fori_loop(0, 16, one, 0)


def grid_kernel(
    images, z_hi_in, z_lo_in, x_hi_in, x_lo_in, lists, slots, weights,
    out, rows_out, turned_out,
    image, z_hi, z_lo, x_hi, x_lo, z_out, x_in, x_out,
    near, near8, listed, mine, mine8, block, turned,
    load_sem, self_sem, send1, recv1, send2, recv2,
    small1, small2, small3, small4, block_sem, turned_sem,
):
    gx, gy = lax.axis_index("gx"), lax.axis_index("gy")
    loads = [
        pltpu.make_async_copy(src, dst, load_sem.at[i])
        for i, (src, dst) in enumerate(
            [(z_hi_in, z_hi), (z_lo_in, z_lo)]
            + [
                (images.at[c, q, :, pl.ds(half * 128, 128)], image.at[half, c, q])
                for c in range(2)
                for q in range(2)
                for half in range(2)
            ]
            + [(x_hi_in, x_hi), (x_lo_in, x_lo)]
        )
    ]
    for load in loads:
        load.start()

    barrier = pltpu.get_barrier_semaphore()
    for r in range(1, GX):
        pl.semaphore_signal(barrier, inc=1, device_id={"gx": (gx + r) % GX})
    for r in range(1, GY):
        pl.semaphore_signal(barrier, inc=1, device_id={"gy": (gy + r) % GY})
    pl.semaphore_wait(barrier, GX + GY - 2)

    def over_x(m, r):
        to = (gx + r) % GX
        return pltpu.make_async_remote_copy(
            src_ref=z_out.at[m, to],
            dst_ref=x_in.at[m, gx],
            send_sem=send1.at[m, r],
            recv_sem=recv1.at[m, r],
            device_id={"gx": to},
        )

    def over_y(m, r):
        to = (gy + r) % GY
        return pltpu.make_async_remote_copy(
            src_ref=x_out.at[m, to],
            dst_ref=out.at[m % 4, gy, pl.ds(m // 4 * 8, 8)],
            send_sem=send2.at[m, r],
            recv_sem=recv2.at[m, r],
            device_id={"gy": to},
        )

    def own_y(m):
        dst = out.at[m % 4, gy, pl.ds(m // 4 * 8, 8)]
        return pltpu.make_async_copy(x_out.at[m, gy], dst, self_sem.at[m])

    hop1 = hops((lambda to: lists, near.at[gx]), "gx", GX, small1)
    hop2 = hops((lambda to: near8, listed.at[gy]), "gy", GY, small2)
    hop3 = hops((lambda to: mine, mine8.at[gx]), "gx", GX, small3)
    hop4 = hops((lambda to: mine8, rows_out.at[gy]), "gy", GY, small4)
    own4 = pltpu.make_async_copy(mine8, rows_out.at[gy], self_sem.at[8])

    def fetch(j, slot):
        src = weights.at[j // 4, :, pl.ds(j % 4 * 128, 128)]
        return pltpu.make_async_copy(src, block.at[slot], block_sem.at[slot])

    def put(j, slot):
        dst = turned_out.at[j // 4, :, pl.ds(j % 4 * 128, 128), :]
        return pltpu.make_async_copy(turned.at[slot], dst, turned_sem.at[slot])

    def z_half(half):
        for c in range(2):
            if half == 0:
                for load in loads[2 + 4 * c : 6 + 4 * c]:
                    load.wait()

            def pair(yp, carry):
                z_pair(yp + 4 * half, c, image, z_hi, z_lo, z_out)
                return carry

            lax.fori_loop(0, 4, pair, 0)

    def send_x(half):
        def one(m, carry):
            for r in range(1, GX):
                over_x(m, r).start()
            return carry

        lax.fori_loop(4 * half, 4 * half + 4, one, 0)

    for hop in hop1:
        hop.start()
    near[gx] = lists[...]
    for load in loads[:2]:
        load.wait()
    z_half(0)
    for hop in hop1:
        hop.wait()
    lane = lax.broadcasted_iota(jnp.int32, (1, 128), 1)
    for a in range(GX):
        kept = jnp.zeros((1, 128), jnp.int32)
        for k in range(4):
            moved = pltpu.roll(near[a, k : k + 1, :], (128 + 16 * k - 16 * gx) % 128, 1)
            kept = jnp.where(lane // 16 == k, moved, kept)
        near8[a : a + 1, :] = kept
    for hop in hop2:
        hop.start()
    listed[gy] = near8[...]
    send_x(0)
    z_half(1)
    for hop in hop2:
        hop.wait()
    own_rows(listed, slots, mine, gy)
    for hop in hop3:
        hop.start()
    mine8[gx] = mine[...]
    send_x(1)
    for slot in range(2):
        fetch(slot, slot).start()
    for load in loads[10:]:
        load.wait()
    for hop in hop3:
        hop.wait()
    for hop in hop4:
        hop.start()
    own4.start()

    def chunk(m, carry):
        slot = m % 2
        fetch(m, slot).wait()

        @pl.when(m > 1)
        def _():
            put(m - 2, slot).wait()

        turn_unit(block.at[slot], turned.at[slot])
        put(m, slot).start()

        @pl.when(m < 6)
        def _():
            fetch(m + 2, slot).start()

        x_in[m, gx] = z_out[m, gx]
        for r in range(1, GX):
            over_x(m, r).wait_recv()
        rows = jnp.concatenate([x_in[m, a].reshape(128, 128) for a in range(8)], 1)
        res = dot3(halves(rows), (x_hi[...], x_lo[...]), ((1,), (0,)))
        for c in range(2):
            for u in range(8):
                x_out[m, c * 8 + u] = res[
                    c * 64 : (c + 1) * 64, u * 128 : (u + 1) * 128
                ].reshape(8, 8, 128)
        for r in range(1, GY):
            over_y(m, r).start()
        own_y(m).start()
        return carry

    lax.fori_loop(0, 8, chunk, 0)
    for hop in hop4:
        hop.wait()
    own4.wait()
    for slot in range(2):
        put(6 + slot, slot).wait()

    def finish(m, carry):
        own_y(m).wait()
        for r in range(1, GX):
            over_x(m, r).wait_send()
        for r in range(1, GY):
            over_y(m, r).wait()
        return carry

    lax.fori_loop(0, 8, finish, 0)


def grid_values(images, lists, slots, weights):
    tables = [jnp.asarray(t) for t in z_table() + x_table()]
    hbm = pl.BlockSpec(memory_space=pltpu.HBM)
    inside = pl.BlockSpec(memory_space=pltpu.VMEM)
    dma = pltpu.SemaphoreType.DMA
    i32 = jnp.int32
    return pl.pallas_call(
        grid_kernel,
        out_shape=(
            jax.ShapeDtypeStruct((4, 16, 16, 8, 128), F32),
            jax.ShapeDtypeStruct((GY, GX, 2, 128), i32),
            jax.ShapeDtypeStruct((2, 16, 512, 128), F32),
        ),
        in_specs=[hbm] * 5 + [inside] * 2 + [hbm],
        out_specs=(hbm,) * 3,
        scratch_shapes=[
            pltpu.VMEM((2, 2, 2, 1024, 128), F32),
            pltpu.VMEM((256, 512), BF16),
            pltpu.VMEM((256, 512), BF16),
            pltpu.VMEM((1024, 1024), BF16),
            pltpu.VMEM((1024, 1024), BF16),
            pltpu.VMEM((8, 8, 2, 8, 8, 128), F32),
            pltpu.VMEM((8, 8, 2, 8, 8, 128), F32),
            pltpu.VMEM((8, 16, 8, 8, 128), F32),
            pltpu.VMEM((GX, 4, 128), i32),
            pltpu.VMEM((GX, 128), i32),
            pltpu.VMEM((GY, GX, 128), i32),
            pltpu.VMEM((2, 128), i32),
            pltpu.VMEM((GX, 2, 128), i32),
            pltpu.VMEM((2, 2048, 128), F32),
            pltpu.VMEM((2, 16, 128, 128), F32),
            dma((12,)),
            dma((9,)),
            dma((8, GX)),
            dma((8, GX)),
            dma((8, GY)),
            dma((8, GY)),
            dma((2, GX)),
            dma((2, GY)),
            dma((2, GX)),
            dma((2, GY)),
            dma((2,)),
            dma((2,)),
        ],
        compiler_params=pltpu.CompilerParams(
            vmem_limit_bytes=WIDE_VMEM, collective_id=0, has_side_effects=True
        ),
        name="grid_values",
    )(images, *tables, lists, slots, weights)


def y_group(g, data, hi, lo, table):
    lane = lax.broadcasted_iota(jnp.int32, (64, 128), 1)

    def four(p, carry):
        rows = []
        for k in range(4):
            turned = data[pl.ds(4 * p + k, 256, stride=8), :].T
            rows.append(jnp.concatenate([turned[:64], turned[64:]], 1))
        res = dot3(halves(jnp.concatenate(rows, 0)), (hi[...], lo[...]), ((1,), (0,)))
        for k in range(4):
            bz = 8 * g + 4 * p + k
            for high in range(4):
                part = res[k * 64 : (k + 1) * 64, high * 128 : (high + 1) * 128]
                for low in range(8):
                    source = low * 16 + jnp.bitwise_and(lane, 15)
                    at = pl.multiple_of((bz * 32 + high * 8 + low) * 64, 64)
                    table[pl.ds(at, 64), :] = jnp.take_along_axis(part, source, axis=1)
        return carry

    lax.fori_loop(0, 2, four, 0)


def pick_group(bases, rows, table, raw, out):
    def eight(t, carry):
        for s in range(8):
            for g in range(8):
                lanes = slice(g * 16, g * 16 + 16)
                row = rows[bases[g] + t * 8 + s]
                raw[pl.ds(t * 8 + s, 1), lanes] = table[pl.ds(row, 1), lanes]
        return carry

    lax.fori_loop(0, 32, eight, 0)
    for h in range(2):
        turned = raw[h * 128 : (h + 1) * 128, :].T
        for g in range(8):
            out[g, h] = turned[g * 16 : (g + 1) * 16]


def pick_kernel(data_in, rows, hi, lo, out, data, table, raw, sent, load_sem, self_sem, send, recv):
    gx, gy = lax.axis_index("gx"), lax.axis_index("gy")
    me = gx * GY + gy
    loads = [
        pltpu.make_async_copy(data_in.at[k], data.at[k], load_sem.at[k]) for k in range(4)
    ]
    for load in loads:
        load.start()
    barrier = pltpu.get_barrier_semaphore()

    def greet(o, carry):
        to = (me + o) % DEVS
        pl.semaphore_signal(barrier, inc=1, device_id={"gx": to // GY, "gy": to % GY})
        return carry

    lax.fori_loop(1, DEVS, greet, 0)

    for k in range(4):
        loads[k].wait()
        y_group(k, data.at[k], hi, lo, table)

    pl.semaphore_wait(barrier, DEVS - 1)

    def copy(i, g):
        return pltpu.make_async_remote_copy(
            src_ref=sent.at[i, g],
            dst_ref=out.at[me],
            send_sem=send.at[i, g],
            recv_sem=recv.at[i, g],
            device_id={"gx": (gx + g) % GX, "gy": (gy + i) % GY},
        )

    own = pltpu.make_async_copy(sent.at[0, 0], out.at[me], self_sem)

    def group(i, carry):
        to = (gy + i) % GY
        bases = [to * 2048 + (gx + g) % GX * 256 for g in range(8)]
        pick_group(bases, rows, table, raw, sent.at[i])

        @pl.when(i == 0)
        def _():
            own.start()

        @pl.when(i > 0)
        def _():
            copy(i, 0).start()

        for g in range(1, 8):
            copy(i, g).start()
        return carry

    lax.fori_loop(0, 16, group, 0)
    own.wait()

    def finish(i, carry):
        @pl.when(i > 0)
        def _():
            copy(i, 0).wait()

        for g in range(1, 8):
            copy(i, g).wait()
        return carry

    lax.fori_loop(0, 16, finish, 0)


def y_pick(data, rows):
    hi, lo = y_table()
    anywhere = pl.BlockSpec(memory_space=pl.ANY)
    inside = pl.BlockSpec(memory_space=pltpu.VMEM)
    dma = pltpu.SemaphoreType.DMA
    return pl.pallas_call(
        pick_kernel,
        out_shape=jax.ShapeDtypeStruct((128, 2, 16, 128), F32),
        in_specs=[anywhere, pl.BlockSpec(memory_space=pltpu.SMEM), inside, inside],
        out_specs=anywhere,
        scratch_shapes=[
            pltpu.VMEM((4, 2048, 128), F32),
            pltpu.VMEM((65536, 128), F32),
            pltpu.VMEM((256, 128), F32),
            pltpu.VMEM((16, 8, 2, 16, 128), F32),
            dma((4,)),
            dma,
            dma((16, 8)),
            dma((16, 8)),
        ],
        compiler_params=pltpu.CompilerParams(
            vmem_limit_bytes=WIDE_VMEM, collective_id=1, has_side_effects=True
        ),
        name="y_pick",
    )(data, rows, jnp.asarray(hi), jnp.asarray(lo))


def sum_kernel(got, weights, out):
    def one(u, carry):
        sums = list(carry)
        for w in range(8):
            at = pl.multiple_of(u * 64 + w * 8, 8)
            factors = [weights[0, n, pl.ds(at, 8), :] for n in range(4)]
            for k in range(4):
                value = got[w, k // 2, u, 0, k % 2]
                for n in range(4):
                    sums[n * 4 + k] = sums[n * 4 + k] + factors[n] * value
        return tuple(sums)

    sums = lax.fori_loop(0, 8, one, (jnp.zeros((8, 128), F32),) * 16)
    rows = [jnp.sum(s, 0, keepdims=True) for s in sums]
    out[0, 0] = jnp.concatenate(rows, 0)


def interpolate(got, weights):
    return pl.pallas_call(
        sum_kernel,
        out_shape=jax.ShapeDtypeStruct((2, 4, 16, 128), F32),
        grid=(2, 4),
        in_specs=[
            pl.BlockSpec((8, 2, 8, 1, 2, 8, 128), lambda h, n: (0, 0, 0, h, 0, 0, 0)),
            pl.BlockSpec((1, 4, 512, 128), lambda h, n: (h, n, 0, 0)),
        ],
        out_specs=pl.BlockSpec((1, 1, 16, 128), lambda h, n: (h, n, 0, 0)),
        compiler_params=pltpu.CompilerParams(vmem_limit_bytes=WIDE_VMEM),
        name="interpolate",
    )(got, weights)


def local(coil_images, send_lists, seg_slots, weights, counts):
    lists = send_lists[0].T
    values, rows, turned = grid_values(
        coil_images.reshape(2, 2, 1024, 256),
        lists,
        seg_slots.reshape(2, 128),
        weights.reshape(2, 2048, 512),
    )
    got = y_pick(values.reshape(4, 2048, 128), rows.reshape(-1))
    sums = interpolate(got.reshape(8, 2, 8, 2, 2, 8, 128), turned)
    sums = sums.reshape(2, 16, 2, 2, 8, 16).sum(-1)
    samples = sums.transpose(0, 4, 2, 3, 1).reshape(16, 2, 2, 16)
    live = jnp.arange(16, dtype=jnp.int32) < counts[:, None, None, None]
    return jnp.where(live, samples, 0.0)


def solution(mesh):
    placed = (
        P(None, None, "gx", "gy", None),
        P(("gx", "gy"), None, None),
        P(("gx", "gy"), None),
        P(("gx", "gy"), None, None, None),
        P(("gx", "gy")),
    )
    return jax.shard_map(
        local,
        mesh=mesh,
        in_specs=placed,
        out_specs=P(("gx", "gy"), None, None, None),
        check_vma=False,
    )
```

```python
import functools
import math

import jax
import jax.numpy as jnp
import numpy as np
from jax import lax
from jax.experimental import pallas as pl
from jax.experimental.pallas import tpu as pltpu
from jax.sharding import PartitionSpec as P

NX, NY, NZ = 512, 256, 256
GX, GY = 8, 16
DEVS = GX * GY
F32, BF16 = jnp.float32, jnp.bfloat16
WIDE_VMEM = 62 * 2**20


def split_table(table):
    hi = table.astype(np.float32).astype(jnp.bfloat16)
    lo = (table - hi.astype(np.float64)).astype(np.float32).astype(jnp.bfloat16)
    return hi, lo


def angle(rows, columns, length):
    return (np.outer(rows, columns) % length) * (2.0 * math.pi / length)


def z_table():
    bz = np.arange(32).reshape(4, 1, 8)
    order = (np.arange(8)[None, :, None] + 8 * bz).reshape(-1)
    phase = angle(order, np.arange(NZ), NZ)
    scale = 1.0 / math.sqrt(NX * NY * NZ)
    return split_table(np.concatenate([np.cos(phase), np.sin(phase)], 1) * scale)


def x_table():
    phase = angle(np.arange(NX), np.arange(NX), NX)
    cos, sin = np.cos(phase), np.sin(phase)
    whole = np.zeros((2, NX, 2, NX))
    whole[0, :, 0], whole[1, :, 0] = cos, sin
    whole[0, :, 1], whole[1, :, 1] = -sin, cos
    whole = whole.reshape(2, 8, 64, 2, 64, 8).transpose(1, 0, 2, 5, 3, 4)
    return split_table(whole.reshape(1024, 1024))


def y_table():
    phase = angle(np.arange(NY), np.arange(NY), NY)
    cos, sin = np.cos(phase), np.sin(phase)
    whole = np.zeros((2, NY, 2, NY))
    whole[0, :, 0], whole[1, :, 0] = cos, sin
    whole[0, :, 1], whole[1, :, 1] = -sin, cos
    whole = whole.reshape(2, NY, 2, 32, 8).transpose(0, 1, 3, 2, 4)
    return split_table(whole.reshape(512, 512))


def halves(value):
    hi = value.astype(BF16)
    return hi, (value - hi.astype(F32)).astype(BF16)


def dot3(left, right, dims):
    def one(a, b):
        return lax.dot_general(a, b, (dims, ((), ())), preferred_element_type=F32)

    return one(left[0], right[0]) + (one(left[0], right[1]) + one(left[1], right[0]))


def z_pair(yp, c, image, hi, lo, sent):
    rows, swapped = [], []
    for k in range(2):
        at = pl.ds(2 * yp + k, 64, stride=16)
        re, im = (
            jnp.concatenate([image[half * 4 + c * 2 + q, at, :] for half in range(2)], 1)
            for q in range(2)
        )
        rows += [re, im]
        swapped += [im, -re]
    data = jnp.concatenate([jnp.concatenate(rows, 0), jnp.concatenate(swapped, 0)], 1)
    res = dot3((hi[...], lo[...]), halves(data), ((1,), (1,)))
    for k in range(2):
        part = res[:, k * 128 : (k + 1) * 128].reshape(4, 8, 8, 128)
        y = 2 * yp + k
        at = pl.multiple_of(c * 64 + y % 8 * 8, 8)
        for b in range(4):
            sent[y // 8 * 4 + b, :, pl.ds(at, 8), :] = part[b]


def hops(pairs, axis, size, sems):
    me = lax.axis_index(axis)
    src, dst = pairs
    made = []
    for r in range(1, size):
        to = (me + r) % size
        made.append(
            pltpu.make_async_remote_copy(
                src_ref=src(to),
                dst_ref=dst,
                send_sem=sems.at[0, r],
                recv_sem=sems.at[1, r],
                device_id={axis: to},
            )
        )
    return made


def own_rows(listed, slots, mine, gy):
    lists = pltpu.roll(listed[...].reshape(128, 128), (128 - gy) % 128, 1)
    row = lax.broadcasted_iota(jnp.int32, (128, 128), 0)
    first = row % 8 * 64 + row // 8 * 4
    for h in range(2):
        wanted = slots[h : h + 1, :]
        total = jnp.zeros((8, 128), jnp.int32)
        for k in range(4):
            column = jnp.broadcast_to(lists[:, 16 * k : 16 * k + 1], (128, 128))
            found = jnp.where(first + k == wanted, column, 0)
            for at in range(0, 128, 8):
                total += found[at : at + 8]
        for by in (4, 2, 1):
            total += pltpu.roll(total, by, 0)
        ids = total[:1]
        bz, by = ids % 32, ids // 32 % 32
        mine[h : h + 1, :] = bz * 2048 + by * 64 + ids // 1024 % 64


def turn_unit(block, turned):
    def one(n, carry):
        part = block[pl.ds(n, 128, stride=16), :].T
        for u in range(2):
            for v in range(8):
                at = (u * 8 + v) * 8
                turned[n, pl.ds(u * 64 + v, 8, stride=8), :] = part[at : at + 8]
        return carry

    lax.fori_loop(0, 16, one, 0)


def y_group(g, data, hi, lo, table):
    lane = lax.broadcasted_iota(jnp.int32, (64, 128), 1)

    def four(p, carry):
        rows = []
        for k in range(4):
            turned = data[pl.ds(4 * p + k, 256, stride=8), :].T
            rows.append(jnp.concatenate([turned[:64], turned[64:]], 1))
        res = dot3(halves(jnp.concatenate(rows, 0)), (hi[...], lo[...]), ((1,), (0,)))
        for k in range(4):
            bz = 8 * g + 4 * p + k
            for high in range(4):
                part = res[k * 64 : (k + 1) * 64, high * 128 : (high + 1) * 128]
                for low in range(8):
                    source = low * 16 + jnp.bitwise_and(lane, 15)
                    at = pl.multiple_of((bz * 32 + high * 8 + low) * 64, 64)
                    table[pl.ds(at, 64), :] = jnp.take_along_axis(part, source, axis=1)
        return carry

    lax.fori_loop(0, 2, four, 0)


def pick_group(to, gx, rows, table, raw):
    owners = [(gx + g) % GX for g in range(8)]

    def eight(t, carry):
        h, first = t // 16, t % 16 * 8
        for s in range(8):
            for g in range(8):
                lanes = slice(g * 16, g * 16 + 16)
                row = rows[to, owners[g], h, first + s]
                raw[pl.ds(t * 8 + s, 1), lanes] = table[pl.ds(row, 1), lanes]
        return carry

    lax.fori_loop(0, 32, eight, 0)


def spread_kernel(
    images, z_hi_in, z_lo_in, x_hi_in, x_lo_in, y_hi_in, y_lo_in, lists, slots, weights,
    out, turned_out,
    x_out, z_hi, z_lo, x_hi, x_lo, y_hi, y_lo, z_out, x_in, y_in, table, raw, rows_all, rows,
    near, near8, listed, mine, mine8, block, turned,
    load_sem, self_sem, send1, recv1, send2, recv2, send3, recv3,
    small1, small2, small3, small4, block_sem, turned_sem, rows_sem,
):
    gx, gy = lax.axis_index("gx"), lax.axis_index("gy")
    me = gx * GY + gy
    image = x_out
    loads = [
        pltpu.make_async_copy(src, dst, load_sem.at[i])
        for i, (src, dst) in enumerate(
            [(z_hi_in, z_hi), (z_lo_in, z_lo)]
            + [
                (images.at[c, q, :, pl.ds(half * 128, 128)], image.at[half * 4 + c * 2 + q])
                for c in range(2)
                for q in range(2)
                for half in range(2)
            ]
            + [(x_hi_in, x_hi), (x_lo_in, x_lo), (y_hi_in, y_hi), (y_lo_in, y_lo)]
        )
    ]
    for load in loads:
        load.start()

    barrier = pltpu.get_barrier_semaphore()
    for r in range(1, GX):
        pl.semaphore_signal(barrier, inc=1, device_id={"gx": (gx + r) % GX})
    for r in range(1, GY):
        pl.semaphore_signal(barrier, inc=1, device_id={"gy": (gy + r) % GY})
    pl.semaphore_wait(barrier, GX + GY - 2)

    def over_x(m, r):
        to = (gx + r) % GX
        return pltpu.make_async_remote_copy(
            src_ref=z_out.at[m, to],
            dst_ref=x_in.at[m, gx],
            send_sem=send1.at[m, r],
            recv_sem=recv1.at[m, r],
            device_id={"gx": to},
        )

    def part_y(m, b):
        return y_in.at[m % 4, pl.ds(pl.multiple_of(b * 128 + m // 4 * 64, 64), 64)]

    def over_y(m, r):
        to = (gy + r) % GY
        return pltpu.make_async_remote_copy(
            src_ref=x_out.at[m, pl.ds(pl.multiple_of(to * 64, 64), 64)],
            dst_ref=part_y(m, gy),
            send_sem=send2.at[m, r],
            recv_sem=recv2.at[m, r],
            device_id={"gy": to},
        )

    def own_y(m):
        src = x_out.at[m, pl.ds(pl.multiple_of(gy * 64, 64), 64)]
        return pltpu.make_async_copy(src, part_y(m, gy), self_sem.at[m])

    def picked(i, g):
        return z_out.at[g, i // 4, pl.ds(pl.multiple_of(i % 4 * 32, 32), 32)]

    def over_all(i, g):
        return pltpu.make_async_remote_copy(
            src_ref=picked(i, g),
            dst_ref=out.at[me],
            send_sem=send3.at[i, g],
            recv_sem=recv3.at[i, g],
            device_id={"gx": (gx + g) % GX, "gy": (gy + i) % GY},
        )

    hop1 = hops((lambda to: lists, near.at[gx]), "gx", GX, small1)
    hop2 = hops((lambda to: near8, listed.at[gy]), "gy", GY, small2)
    hop3 = hops((lambda to: mine, mine8.at[gx]), "gx", GX, small3)
    hop4 = hops((lambda to: mine8, rows_all.at[gy]), "gy", GY, small4)
    to_scalars = pltpu.make_async_copy(rows_all, rows, rows_sem)
    own = pltpu.make_async_copy(picked(0, 0), out.at[me], self_sem.at[8])

    def fetch(j, slot):
        src = weights.at[j // 4, :, pl.ds(j % 4 * 128, 128)]
        return pltpu.make_async_copy(src, block.at[slot], block_sem.at[slot])

    def put(j, slot):
        dst = turned_out.at[j // 4, :, pl.ds(j % 4 * 128, 128), :]
        return pltpu.make_async_copy(turned.at[slot], dst, turned_sem.at[slot])

    def z_half(half):
        for c in range(2):
            if half == 0:
                for load in loads[2 + 4 * c : 6 + 4 * c]:
                    load.wait()

            def pair(yp, carry):
                z_pair(yp + 4 * half, c, image, z_hi, z_lo, z_out)
                return carry

            lax.fori_loop(0, 4, pair, 0)

    def send_x(half):
        def one(m, carry):
            for r in range(1, GX):
                over_x(m, r).start()
            return carry

        lax.fori_loop(4 * half, 4 * half + 4, one, 0)

    for hop in hop1:
        hop.start()
    near[gx] = lists[...]
    for load in loads[:2]:
        load.wait()
    z_half(0)
    send_x(0)
    z_half(1)
    send_x(1)
    for slot in range(2):
        fetch(slot, slot).start()
    for hop in hop1:
        hop.wait()
    lane = lax.broadcasted_iota(jnp.int32, (1, 128), 1)
    for a in range(GX):
        kept = jnp.zeros((1, 128), jnp.int32)
        for k in range(4):
            moved = pltpu.roll(near[a, k : k + 1, :], (128 + 16 * k - 16 * gx) % 128, 1)
            kept = jnp.where(lane // 16 == k, moved, kept)
        near8[a : a + 1, :] = kept
    for hop in hop2:
        hop.start()
    listed[gy] = near8[...]
    for load in loads[10:]:
        load.wait()

    def chunk(m, carry):
        slot = m % 2
        fetch(m, slot).wait()

        @pl.when(m > 1)
        def _():
            put(m - 2, slot).wait()

        turn_unit(block.at[slot], turned.at[slot])
        put(m, slot).start()

        @pl.when(m < 6)
        def _():
            fetch(m + 2, slot).start()

        x_in[m, gx] = z_out[m, gx]
        for r in range(1, GX):
            over_x(m, r).wait_recv()
        both = jnp.concatenate([x_in[m, a] for a in range(8)], 1)
        res = dot3(halves(both), (x_hi[...], x_lo[...]), ((1,), (0,)))
        for c in range(2):
            for u in range(8):
                at = (c * 8 + u) * 64
                x_out[m, at : at + 64] = res[
                    c * 64 : (c + 1) * 64, u * 128 : (u + 1) * 128
                ]
        for r in range(1, GY):
            over_y(m, r).start()
        own_y(m).start()

        @pl.when(m == 2)
        def _():
            for hop in hop2:
                hop.wait()
            own_rows(listed, slots, mine, gy)
            for hop in hop3:
                hop.start()
            mine8[gx] = mine[...]

        @pl.when(m == 4)
        def _():
            for hop in hop3:
                hop.wait()
            for hop in hop4:
                hop.start()
            rows_all[gy] = mine8[...]

        return carry

    lax.fori_loop(0, 8, chunk, 0)

    def group_y(k, carry):
        for m in (k, k + 4):
            own_y(m).wait()
            for r in range(1, GY):
                over_y(m, r).wait_recv()
        y_group(k, y_in.at[k], y_hi, y_lo, table)
        return carry

    def sent_x(m, carry):
        for r in range(1, GX):
            over_x(m, r).wait_send()
        return carry

    lax.fori_loop(0, 8, sent_x, 0)
    for hop in hop4:
        hop.wait()
    to_scalars.start()
    for slot in range(2):
        put(6 + slot, slot).wait()
    lax.fori_loop(0, 4, group_y, 0)
    to_scalars.wait()

    def group(i, carry):
        to = (gy + i) % GY
        pick_group(to, gx, rows, table, raw)
        for h in range(2):
            turned_raw = raw[h * 128 : (h + 1) * 128, :].T
            for g in range(8):
                at = pl.multiple_of(i % 4 * 32 + h * 16, 16)
                part = turned_raw[g * 16 : (g + 1) * 16]
                z_out[g, i // 4, pl.ds(at, 16), :] = part

        @pl.when(i == 0)
        def _():
            own.start()

        @pl.when(i > 0)
        def _():
            over_all(i, 0).start()

        for g in range(1, 8):
            over_all(i, g).start()
        return carry

    lax.fori_loop(0, 16, group, 0)
    own.wait()

    def finish(m, carry):
        for r in range(1, GY):
            over_y(m, r).wait_send()
        return carry

    lax.fori_loop(0, 8, finish, 0)

    def finish_all(i, carry):
        @pl.when(i > 0)
        def _():
            over_all(i, 0).wait()

        for g in range(1, 8):
            over_all(i, g).wait()
        return carry

    lax.fori_loop(0, 16, finish_all, 0)


def spread(images, lists, slots, weights):
    tables = [jnp.asarray(t) for t in z_table() + x_table() + y_table()]
    hbm = pl.BlockSpec(memory_space=pltpu.HBM)
    inside = pl.BlockSpec(memory_space=pltpu.VMEM)
    dma = pltpu.SemaphoreType.DMA
    i32 = jnp.int32
    return pl.pallas_call(
        spread_kernel,
        out_shape=(
            jax.ShapeDtypeStruct((DEVS, 32, 128), F32),
            jax.ShapeDtypeStruct((2, 16, 512, 128), F32),
        ),
        in_specs=[hbm] * 7 + [inside] * 2 + [hbm],
        out_specs=(hbm,) * 2,
        scratch_shapes=[
            pltpu.VMEM((8, 1024, 128), F32),
            pltpu.VMEM((256, 512), BF16),
            pltpu.VMEM((256, 512), BF16),
            pltpu.VMEM((1024, 1024), BF16),
            pltpu.VMEM((1024, 1024), BF16),
            pltpu.VMEM((512, 512), BF16),
            pltpu.VMEM((512, 512), BF16),
            pltpu.VMEM((8, 8, 128, 128), F32),
            pltpu.VMEM((8, 8, 128, 128), F32),
            pltpu.VMEM((4, 2048, 128), F32),
            pltpu.VMEM((65536, 128), F32),
            pltpu.VMEM((256, 128), F32),
            pltpu.VMEM((GY, GX, 2, 128), i32),
            pltpu.SMEM((GY, GX, 2, 128), i32),
            pltpu.VMEM((GX, 4, 128), i32),
            pltpu.VMEM((GX, 128), i32),
            pltpu.VMEM((GY, GX, 128), i32),
            pltpu.VMEM((2, 128), i32),
            pltpu.VMEM((GX, 2, 128), i32),
            pltpu.VMEM((2, 2048, 128), F32),
            pltpu.VMEM((2, 16, 128, 128), F32),
            dma((14,)),
            dma((9,)),
            dma((8, GX)),
            dma((8, GX)),
            dma((8, GY)),
            dma((8, GY)),
            dma((16, 8)),
            dma((16, 8)),
            dma((2, GX)),
            dma((2, GY)),
            dma((2, GX)),
            dma((2, GY)),
            dma((2,)),
            dma((2,)),
            dma,
        ],
        compiler_params=pltpu.CompilerParams(
            vmem_limit_bytes=WIDE_VMEM, collective_id=0, has_side_effects=True
        ),
        name="spread",
    )(images, *tables, lists, slots, weights)


def sum_kernel(got, weights, out):
    def one(u, carry):
        sums = list(carry)
        for w in range(8):
            at = pl.multiple_of(u * 64 + w * 8, 8)
            factors = [weights[0, n, pl.ds(at, 8), :] for n in range(4)]
            for k in range(4):
                value = got[w, k // 2, u, 0, k % 2]
                for n in range(4):
                    sums[n * 4 + k] = sums[n * 4 + k] + factors[n] * value
        return tuple(sums)

    sums = lax.fori_loop(0, 8, one, (jnp.zeros((8, 128), F32),) * 16)
    rows = [jnp.sum(s, 0, keepdims=True) for s in sums]
    out[0, 0] = jnp.concatenate(rows, 0)


def interpolate(got, weights):
    return pl.pallas_call(
        sum_kernel,
        out_shape=jax.ShapeDtypeStruct((2, 4, 16, 128), F32),
        grid=(2, 4),
        in_specs=[
            pl.BlockSpec((8, 2, 8, 1, 2, 8, 128), lambda h, n: (0, 0, 0, h, 0, 0, 0)),
            pl.BlockSpec((1, 4, 512, 128), lambda h, n: (h, n, 0, 0)),
        ],
        out_specs=pl.BlockSpec((1, 1, 16, 128), lambda h, n: (h, n, 0, 0)),
        compiler_params=pltpu.CompilerParams(vmem_limit_bytes=WIDE_VMEM),
        name="interpolate",
    )(got, weights)


def local(coil_images, send_lists, seg_slots, weights, counts):
    lists = send_lists[0].T
    got, turned = spread(
        coil_images.reshape(2, 2, 1024, 256),
        lists,
        seg_slots.reshape(2, 128),
        weights.reshape(2, 2048, 512),
    )
    sums = interpolate(got.reshape(8, 2, 8, 2, 2, 8, 128), turned)
    sums = sums.reshape(2, 16, 2, 2, 8, 16).sum(-1)
    samples = sums.transpose(0, 4, 2, 3, 1).reshape(16, 2, 2, 16)
    live = jnp.arange(16, dtype=jnp.int32) < counts[:, None, None, None]
    return jnp.where(live, samples, 0.0)


def solution(mesh):
    placed = (
        P(None, None, "gx", "gy", None),
        P(("gx", "gy"), None, None),
        P(("gx", "gy"), None),
        P(("gx", "gy"), None, None, None),
        P(("gx", "gy")),
    )
    return jax.shard_map(
        local,
        mesh=mesh,
        in_specs=placed,
        out_specs=P(("gx", "gy"), None, None, None),
        check_vma=False,
    )
```

```python
import functools
import math

import jax
import jax.numpy as jnp
import numpy as np
from jax import lax
from jax.experimental import pallas as pl
from jax.experimental.pallas import tpu as pltpu
from jax.sharding import PartitionSpec as P

NX, NY, NZ = 512, 256, 256
GX, GY = 8, 16
DEVS = GX * GY
F32, BF16 = jnp.float32, jnp.bfloat16
WIDE_VMEM = 62 * 2**20


def split_table(table):
    hi = table.astype(np.float32).astype(jnp.bfloat16)
    lo = (table - hi.astype(np.float64)).astype(np.float32).astype(jnp.bfloat16)
    return hi, lo


def angle(rows, columns, length):
    return (np.outer(rows, columns) % length) * (2.0 * math.pi / length)


def z_table():
    bz = np.arange(32).reshape(4, 1, 8)
    order = (np.arange(8)[None, :, None] + 8 * bz).reshape(-1)
    phase = angle(order, np.arange(NZ), NZ)
    scale = 1.0 / math.sqrt(NX * NY * NZ)
    return split_table(np.concatenate([np.cos(phase), np.sin(phase)], 1) * scale)


def x_table():
    phase = angle(np.arange(NX), np.arange(NX), NX)
    cos, sin = np.cos(phase), np.sin(phase)
    whole = np.zeros((2, NX, 2, NX))
    whole[0, :, 0], whole[1, :, 0] = cos, sin
    whole[0, :, 1], whole[1, :, 1] = -sin, cos
    whole = whole.reshape(2, 8, 64, 2, 64, 8).transpose(1, 0, 2, 5, 3, 4)
    return split_table(whole.reshape(1024, 1024))


def y_table():
    phase = angle(np.arange(NY), np.arange(NY), NY)
    cos, sin = np.cos(phase), np.sin(phase)
    whole = np.zeros((2, NY, 2, NY))
    whole[0, :, 0], whole[1, :, 0] = cos, sin
    whole[0, :, 1], whole[1, :, 1] = -sin, cos
    whole = whole.reshape(2, NY, 2, 32, 8).transpose(0, 1, 3, 2, 4)
    return split_table(whole.reshape(512, 512))


def halves(value):
    hi = value.astype(BF16)
    return hi, (value - hi.astype(F32)).astype(BF16)


def dot3(left, right, dims):
    def one(a, b):
        return lax.dot_general(a, b, (dims, ((), ())), preferred_element_type=F32)

    return one(left[0], right[0]) + (one(left[0], right[1]) + one(left[1], right[0]))


def z_pair(yp, c, image, hi, lo, sent):
    rows, swapped = [], []
    for k in range(2):
        at = pl.ds(2 * yp + k, 64, stride=16)
        re, im = (
            jnp.concatenate([image[half * 4 + c * 2 + q, at, :] for half in range(2)], 1)
            for q in range(2)
        )
        rows += [re, im]
        swapped += [im, -re]
    data = jnp.concatenate([jnp.concatenate(rows, 0), jnp.concatenate(swapped, 0)], 1)
    res = dot3((hi[...], lo[...]), halves(data), ((1,), (1,)))
    for k in range(2):
        part = res[:, k * 128 : (k + 1) * 128].reshape(4, 8, 8, 128)
        y = 2 * yp + k
        at = pl.multiple_of(c * 64 + y % 8 * 8, 8)
        for b in range(4):
            sent[y // 8 * 4 + b, :, pl.ds(at, 8), :] = part[b]


def hops(pairs, axis, size, sems):
    me = lax.axis_index(axis)
    src, dst = pairs
    made = []
    for r in range(1, size):
        to = (me + r) % size
        made.append(
            pltpu.make_async_remote_copy(
                src_ref=src(to),
                dst_ref=dst,
                send_sem=sems.at[0, r],
                recv_sem=sems.at[1, r],
                device_id={axis: to},
            )
        )
    return made


def own_rows(listed, slots, mine, gy):
    lists = pltpu.roll(listed[...].reshape(128, 128), (128 - gy) % 128, 1)
    row = lax.broadcasted_iota(jnp.int32, (128, 128), 0)
    first = row % 8 * 64 + row // 8 * 4
    for h in range(2):
        wanted = slots[h : h + 1, :]
        total = jnp.zeros((8, 128), jnp.int32)
        for k in range(4):
            column = jnp.broadcast_to(lists[:, 16 * k : 16 * k + 1], (128, 128))
            found = jnp.where(first + k == wanted, column, 0)
            for at in range(0, 128, 8):
                total += found[at : at + 8]
        for by in (4, 2, 1):
            total += pltpu.roll(total, by, 0)
        ids = total[:1]
        bz, by = ids % 32, ids // 32 % 32
        mine[h : h + 1, :] = bz * 2048 + by * 64 + ids // 1024 % 64


def turn_unit(block, turned):
    def one(n, carry):
        part = block[pl.ds(n, 128, stride=16), :].T
        for u in range(2):
            for v in range(8):
                at = (u * 8 + v) * 8
                turned[n, pl.ds(u * 64 + v, 8, stride=8), :] = part[at : at + 8]
        return carry

    lax.fori_loop(0, 16, one, 0)


def y_group(g, data, hi, lo, table):
    lane = lax.broadcasted_iota(jnp.int32, (64, 128), 1)

    def four(p, carry):
        rows = []
        for k in range(4):
            turned = data[pl.ds(4 * p + k, 256, stride=8), :].T
            rows.append(jnp.concatenate([turned[:64], turned[64:]], 1))
        res = dot3(halves(jnp.concatenate(rows, 0)), (hi[...], lo[...]), ((1,), (0,)))
        for k in range(4):
            bz = 8 * g + 4 * p + k
            for high in range(4):
                part = res[k * 64 : (k + 1) * 64, high * 128 : (high + 1) * 128]
                for low in range(8):
                    source = low * 16 + jnp.bitwise_and(lane, 15)
                    at = pl.multiple_of((bz * 32 + high * 8 + low) * 64, 64)
                    table[pl.ds(at, 64), :] = jnp.take_along_axis(part, source, axis=1)
        return carry

    lax.fori_loop(0, 2, four, 0)


def pick_group(to, gx, rows, table, raw):
    owners = [(gx + g) % GX for g in range(8)]

    def eight(t, carry):
        h, first = t // 16, t % 16 * 8
        views = [rows.at[to, owners[g], h] for g in range(8)]
        for s in range(8):
            for g in range(8):
                lanes = slice(g * 16, g * 16 + 16)
                row = views[g][first + s]
                raw[pl.ds(t * 8 + s, 1), lanes] = table[pl.ds(row, 1), lanes]
        return carry

    lax.fori_loop(0, 32, eight, 0)


def spread_kernel(
    images, z_hi_in, z_lo_in, x_hi_in, x_lo_in, y_hi_in, y_lo_in, lists, slots, weights,
    out, turned_out,
    x_out, z_hi, z_lo, x_hi, x_lo, y_hi, y_lo, z_out, x_in, y_in, table, raw, rows_all, rows,
    near, near8, listed, mine, mine8, block, turned,
    load_sem, self_sem, send1, recv1, send2, recv2, send3, recv3,
    small1, small2, small3, small4, block_sem, turned_sem, rows_sem,
):
    gx, gy = lax.axis_index("gx"), lax.axis_index("gy")
    me = gx * GY + gy
    image = x_out
    loads = [
        pltpu.make_async_copy(src, dst, load_sem.at[i])
        for i, (src, dst) in enumerate(
            [(z_hi_in, z_hi), (z_lo_in, z_lo)]
            + [
                (images.at[c, q, :, pl.ds(half * 128, 128)], image.at[half * 4 + c * 2 + q])
                for c in range(2)
                for q in range(2)
                for half in range(2)
            ]
            + [(x_hi_in, x_hi), (x_lo_in, x_lo), (y_hi_in, y_hi), (y_lo_in, y_lo)]
        )
    ]
    for load in loads:
        load.start()

    barrier = pltpu.get_barrier_semaphore()
    for r in range(1, GX):
        pl.semaphore_signal(barrier, inc=1, device_id={"gx": (gx + r) % GX})
    for r in range(1, GY):
        pl.semaphore_signal(barrier, inc=1, device_id={"gy": (gy + r) % GY})
    pl.semaphore_wait(barrier, GX + GY - 2)

    def over_x(m, r):
        to = (gx + r) % GX
        return pltpu.make_async_remote_copy(
            src_ref=z_out.at[m, to],
            dst_ref=x_in.at[m, gx],
            send_sem=send1.at[m, r],
            recv_sem=recv1.at[m, r],
            device_id={"gx": to},
        )

    def part_y(m, b):
        return y_in.at[m % 4, pl.ds(pl.multiple_of(b * 128 + m // 4 * 64, 64), 64)]

    def over_y(m, r):
        to = (gy + r) % GY
        return pltpu.make_async_remote_copy(
            src_ref=x_out.at[m, pl.ds(pl.multiple_of(to * 64, 64), 64)],
            dst_ref=part_y(m, gy),
            send_sem=send2.at[m, r],
            recv_sem=recv2.at[m, r],
            device_id={"gy": to},
        )

    def own_y(m):
        src = x_out.at[m, pl.ds(pl.multiple_of(gy * 64, 64), 64)]
        return pltpu.make_async_copy(src, part_y(m, gy), self_sem.at[m])

    def picked(i, g):
        return z_out.at[g, i // 4, pl.ds(pl.multiple_of(i % 4 * 32, 32), 32)]

    def over_all(i, g):
        return pltpu.make_async_remote_copy(
            src_ref=picked(i, g),
            dst_ref=out.at[me],
            send_sem=send3.at[i, g],
            recv_sem=recv3.at[i, g],
            device_id={"gx": (gx + g) % GX, "gy": (gy + i) % GY},
        )

    hop1 = hops((lambda to: lists, near.at[gx]), "gx", GX, small1)
    hop2 = hops((lambda to: near8, listed.at[gy]), "gy", GY, small2)
    hop3 = hops((lambda to: mine, mine8.at[gx]), "gx", GX, small3)
    hop4 = hops((lambda to: mine8, rows_all.at[gy]), "gy", GY, small4)
    to_scalars = pltpu.make_async_copy(rows_all, rows, rows_sem)
    own = pltpu.make_async_copy(picked(0, 0), out.at[me], self_sem.at[8])

    def fetch(j, slot):
        src = weights.at[j // 4, :, pl.ds(j % 4 * 128, 128)]
        return pltpu.make_async_copy(src, block.at[slot], block_sem.at[slot])

    def put(j, slot):
        dst = turned_out.at[j // 4, :, pl.ds(j % 4 * 128, 128), :]
        return pltpu.make_async_copy(turned.at[slot], dst, turned_sem.at[slot])

    def z_half(half):
        for c in range(2):
            if half == 0:
                for load in loads[2 + 4 * c : 6 + 4 * c]:
                    load.wait()

            def pair(yp, carry):
                z_pair(yp + 4 * half, c, image, z_hi, z_lo, z_out)
                return carry

            lax.fori_loop(0, 4, pair, 0)

    def send_x(half):
        def one(m, carry):
            for r in range(1, GX):
                over_x(m, r).start()
            return carry

        lax.fori_loop(4 * half, 4 * half + 4, one, 0)

    for hop in hop1:
        hop.start()
    near[gx] = lists[...]
    for load in loads[:2]:
        load.wait()
    z_half(0)
    send_x(0)
    z_half(1)
    send_x(1)
    for slot in range(2):
        fetch(slot, slot).start()
    for hop in hop1:
        hop.wait()
    lane = lax.broadcasted_iota(jnp.int32, (1, 128), 1)
    for a in range(GX):
        kept = jnp.zeros((1, 128), jnp.int32)
        for k in range(4):
            moved = pltpu.roll(near[a, k : k + 1, :], (128 + 16 * k - 16 * gx) % 128, 1)
            kept = jnp.where(lane // 16 == k, moved, kept)
        near8[a : a + 1, :] = kept
    for hop in hop2:
        hop.start()
    listed[gy] = near8[...]
    for load in loads[10:]:
        load.wait()

    def chunk(m, carry):
        slot = m % 2
        fetch(m, slot).wait()

        @pl.when(m > 1)
        def _():
            put(m - 2, slot).wait()

        turn_unit(block.at[slot], turned.at[slot])
        put(m, slot).start()

        @pl.when(m < 6)
        def _():
            fetch(m + 2, slot).start()

        x_in[m, gx] = z_out[m, gx]
        for r in range(1, GX):
            over_x(m, r).wait_recv()
        both = jnp.concatenate([x_in[m, a] for a in range(8)], 1)
        res = dot3(halves(both), (x_hi[...], x_lo[...]), ((1,), (0,)))
        for c in range(2):
            for u in range(8):
                at = (c * 8 + u) * 64
                x_out[m, at : at + 64] = res[
                    c * 64 : (c + 1) * 64, u * 128 : (u + 1) * 128
                ]
        for r in range(1, GY):
            over_y(m, r).start()
        own_y(m).start()

        @pl.when(m == 2)
        def _():
            for hop in hop2:
                hop.wait()
            own_rows(listed, slots, mine, gy)
            for hop in hop3:
                hop.start()
            mine8[gx] = mine[...]

        @pl.when(m == 4)
        def _():
            for hop in hop3:
                hop.wait()
            for hop in hop4:
                hop.start()
            rows_all[gy] = mine8[...]

        return carry

    lax.fori_loop(0, 8, chunk, 0)

    def group_y(k, carry):
        for m in (k, k + 4):
            own_y(m).wait()
            for r in range(1, GY):
                over_y(m, r).wait_recv()
        y_group(k, y_in.at[k], y_hi, y_lo, table)
        return carry

    def sent_x(m, carry):
        for r in range(1, GX):
            over_x(m, r).wait_send()
        return carry

    lax.fori_loop(0, 8, sent_x, 0)
    for hop in hop4:
        hop.wait()
    to_scalars.start()
    for slot in range(2):
        put(6 + slot, slot).wait()
    lax.fori_loop(0, 4, group_y, 0)
    to_scalars.wait()

    def group(i, carry):
        to = (gy + i) % GY
        pick_group(to, gx, rows, table, raw)
        for h in range(2):
            turned_raw = raw[h * 128 : (h + 1) * 128, :].T
            for g in range(8):
                at = pl.multiple_of(i % 4 * 32 + h * 16, 16)
                part = turned_raw[g * 16 : (g + 1) * 16]
                z_out[g, i // 4, pl.ds(at, 16), :] = part

        @pl.when(i == 0)
        def _():
            own.start()

        @pl.when(i > 0)
        def _():
            over_all(i, 0).start()

        for g in range(1, 8):
            over_all(i, g).start()
        return carry

    lax.fori_loop(0, 16, group, 0)
    own.wait()

    def finish(m, carry):
        for r in range(1, GY):
            over_y(m, r).wait_send()
        return carry

    lax.fori_loop(0, 8, finish, 0)

    def finish_all(i, carry):
        @pl.when(i > 0)
        def _():
            over_all(i, 0).wait()

        for g in range(1, 8):
            over_all(i, g).wait()
        return carry

    lax.fori_loop(0, 16, finish_all, 0)


def spread(images, lists, slots, weights):
    tables = [jnp.asarray(t) for t in z_table() + x_table() + y_table()]
    hbm = pl.BlockSpec(memory_space=pltpu.HBM)
    inside = pl.BlockSpec(memory_space=pltpu.VMEM)
    dma = pltpu.SemaphoreType.DMA
    i32 = jnp.int32
    return pl.pallas_call(
        spread_kernel,
        out_shape=(
            jax.ShapeDtypeStruct((DEVS, 32, 128), F32),
            jax.ShapeDtypeStruct((2, 16, 512, 128), F32),
        ),
        in_specs=[hbm] * 7 + [inside] * 2 + [hbm],
        out_specs=(hbm,) * 2,
        scratch_shapes=[
            pltpu.VMEM((8, 1024, 128), F32),
            pltpu.VMEM((256, 512), BF16),
            pltpu.VMEM((256, 512), BF16),
            pltpu.VMEM((1024, 1024), BF16),
            pltpu.VMEM((1024, 1024), BF16),
            pltpu.VMEM((512, 512), BF16),
            pltpu.VMEM((512, 512), BF16),
            pltpu.VMEM((8, 8, 128, 128), F32),
            pltpu.VMEM((8, 8, 128, 128), F32),
            pltpu.VMEM((4, 2048, 128), F32),
            pltpu.VMEM((65536, 128), F32),
            pltpu.VMEM((256, 128), F32),
            pltpu.VMEM((GY, GX, 2, 128), i32),
            pltpu.SMEM((GY, GX, 2, 128), i32),
            pltpu.VMEM((GX, 4, 128), i32),
            pltpu.VMEM((GX, 128), i32),
            pltpu.VMEM((GY, GX, 128), i32),
            pltpu.VMEM((2, 128), i32),
            pltpu.VMEM((GX, 2, 128), i32),
            pltpu.VMEM((2, 2048, 128), F32),
            pltpu.VMEM((2, 16, 128, 128), F32),
            dma((14,)),
            dma((9,)),
            dma((8, GX)),
            dma((8, GX)),
            dma((8, GY)),
            dma((8, GY)),
            dma((16, 8)),
            dma((16, 8)),
            dma((2, GX)),
            dma((2, GY)),
            dma((2, GX)),
            dma((2, GY)),
            dma((2,)),
            dma((2,)),
            dma,
        ],
        compiler_params=pltpu.CompilerParams(
            vmem_limit_bytes=WIDE_VMEM, collective_id=0, has_side_effects=True
        ),
        name="spread",
    )(images, *tables, lists, slots, weights)


def sum_kernel(got, weights, out):
    rows = []
    for half in range(2):

        def one(u, carry):
            sums = list(carry)
            for w in range(8):
                at = pl.multiple_of(u * 64 + w * 8, 8)
                factors = [weights[0, 4 * half + n, pl.ds(at, 8), :] for n in range(4)]
                for k in range(4):
                    value = got[w, k // 2, u, 0, k % 2]
                    for n in range(4):
                        sums[n * 4 + k] = sums[n * 4 + k] + factors[n] * value
            return tuple(sums)

        sums = lax.fori_loop(0, 8, one, (jnp.zeros((8, 128), F32),) * 16)
        rows += [jnp.sum(s, 0, keepdims=True) for s in sums]
    lane = lax.broadcasted_iota(jnp.int32, (8, 128), 1)
    owner = lax.broadcasted_iota(jnp.int32, (8, 128), 0)
    ones = jnp.where(lane // 16 == owner, 1.0, 0.0)
    out[0, 0] = lax.dot_general(
        ones,
        jnp.concatenate(rows, 0),
        (((1,), (1,)), ((), ())),
        precision=lax.Precision.HIGHEST,
        preferred_element_type=F32,
    )


def interpolate(got, weights):
    return pl.pallas_call(
        sum_kernel,
        out_shape=jax.ShapeDtypeStruct((2, 2, 8, 32), F32),
        grid=(2, 2),
        in_specs=[
            pl.BlockSpec((8, 2, 8, 1, 2, 8, 128), lambda h, n: (0, 0, 0, h, 0, 0, 0)),
            pl.BlockSpec((1, 8, 512, 128), lambda h, n: (h, n, 0, 0)),
        ],
        out_specs=pl.BlockSpec((1, 1, 8, 32), lambda h, n: (h, n, 0, 0)),
        compiler_params=pltpu.CompilerParams(vmem_limit_bytes=WIDE_VMEM),
        name="interpolate",
    )(got, weights)


def local(coil_images, send_lists, seg_slots, weights, counts):
    lists = send_lists[0].T
    got, turned = spread(
        coil_images.reshape(2, 2, 1024, 256),
        lists,
        seg_slots.reshape(2, 128),
        weights.reshape(2, 2048, 512),
    )
    sums = interpolate(got.reshape(8, 2, 8, 2, 2, 8, 128), turned)
    samples = sums.reshape(2, 2, 8, 8, 2, 2).transpose(0, 2, 4, 5, 1, 3)
    samples = samples.reshape(16, 2, 2, 16)
    live = jnp.arange(16, dtype=jnp.int32) < counts[:, None, None, None]
    return jnp.where(live, samples, 0.0)


def solution(mesh):
    placed = (
        P(None, None, "gx", "gy", None),
        P(("gx", "gy"), None, None),
        P(("gx", "gy"), None),
        P(("gx", "gy"), None, None, None),
        P(("gx", "gy")),
    )
    return jax.shard_map(
        local,
        mesh=mesh,
        in_specs=placed,
        out_specs=P(("gx", "gy"), None, None, None),
        check_vma=False,
    )
```

```python
import functools
import math

import jax
import jax.numpy as jnp
import numpy as np
from jax import lax
from jax.experimental import pallas as pl
from jax.experimental.pallas import tpu as pltpu
from jax.sharding import PartitionSpec as P

NX, NY, NZ = 512, 256, 256
GX, GY = 8, 16
DEVS = GX * GY
F32, BF16 = jnp.float32, jnp.bfloat16
WIDE_VMEM = 62 * 2**20


def split_table(table):
    hi = table.astype(np.float32).astype(jnp.bfloat16)
    lo = (table - hi.astype(np.float64)).astype(np.float32).astype(jnp.bfloat16)
    return hi, lo


def angle(rows, columns, length):
    return (np.outer(rows, columns) % length) * (2.0 * math.pi / length)


def z_table():
    bz = np.arange(32).reshape(4, 1, 8)
    order = (np.arange(8)[None, :, None] + 8 * bz).reshape(-1)
    phase = angle(order, np.arange(NZ), NZ)
    scale = 1.0 / math.sqrt(NX * NY * NZ)
    return split_table(np.concatenate([np.cos(phase), np.sin(phase)], 1) * scale)


def x_table():
    phase = angle(np.arange(NX), np.arange(NX), NX)
    cos, sin = np.cos(phase), np.sin(phase)
    whole = np.zeros((2, NX, 2, NX))
    whole[0, :, 0], whole[1, :, 0] = cos, sin
    whole[0, :, 1], whole[1, :, 1] = -sin, cos
    whole = whole.reshape(2, 8, 64, 2, 64, 8).transpose(1, 0, 2, 5, 3, 4)
    return split_table(whole.reshape(1024, 1024))


def y_table():
    phase = angle(np.arange(NY), np.arange(NY), NY)
    cos, sin = np.cos(phase), np.sin(phase)
    whole = np.zeros((2, NY, 2, NY))
    whole[0, :, 0], whole[1, :, 0] = cos, sin
    whole[0, :, 1], whole[1, :, 1] = -sin, cos
    whole = whole.reshape(2, NY, 2, 32, 8).transpose(0, 1, 3, 2, 4)
    return split_table(whole.reshape(512, 512))


def halves(value):
    hi = value.astype(BF16)
    return hi, (value - hi.astype(F32)).astype(BF16)


def dot3(left, right, dims):
    def one(a, b):
        return lax.dot_general(a, b, (dims, ((), ())), preferred_element_type=F32)

    return one(left[0], right[0]) + (one(left[0], right[1]) + one(left[1], right[0]))


def z_pair(yp, c, image, hi, lo, sent):
    rows, swapped = [], []
    for k in range(2):
        at = pl.ds(2 * yp + k, 64, stride=16)
        re, im = (
            jnp.concatenate([image[half * 4 + c * 2 + q, at, :] for half in range(2)], 1)
            for q in range(2)
        )
        rows += [re, im]
        swapped += [im, -re]
    data = jnp.concatenate([jnp.concatenate(rows, 0), jnp.concatenate(swapped, 0)], 1)
    res = dot3((hi[...], lo[...]), halves(data), ((1,), (1,)))
    for k in range(2):
        part = res[:, k * 128 : (k + 1) * 128].reshape(4, 8, 8, 128)
        y = 2 * yp + k
        at = pl.multiple_of(c * 64 + y % 8 * 8, 8)
        for b in range(4):
            sent[y // 8 * 4 + b, :, pl.ds(at, 8), :] = part[b]


def hops(pairs, axis, size, sems):
    me = lax.axis_index(axis)
    src, dst = pairs
    made = []
    for r in range(1, size):
        to = (me + r) % size
        made.append(
            pltpu.make_async_remote_copy(
                src_ref=src(to),
                dst_ref=dst,
                send_sem=sems.at[0, r],
                recv_sem=sems.at[1, r],
                device_id={axis: to},
            )
        )
    return made


def own_rows(listed, slots, mine, gy):
    lists = pltpu.roll(listed[...].reshape(128, 128), (128 - gy) % 128, 1)
    row = lax.broadcasted_iota(jnp.int32, (128, 128), 0)
    first = row % 8 * 64 + row // 8 * 4
    lane = lax.broadcasted_iota(jnp.int32, (1, 128), 1)
    for h in range(2):
        wanted = jnp.zeros((1, 128), jnp.int32)
        for at in range(8):
            moved = slots[h * 8 + at : h * 8 + at + 1, :]
            if at > 0:
                moved = pltpu.roll(moved, 16 * at, 1)
            wanted = jnp.where(lane // 16 == at, moved, wanted)
        total = jnp.zeros((8, 128), jnp.int32)
        for k in range(4):
            column = jnp.broadcast_to(lists[:, 16 * k : 16 * k + 1], (128, 128))
            found = jnp.where(first + k == wanted, column, 0)
            for at in range(0, 128, 8):
                total += found[at : at + 8]
        for by in (4, 2, 1):
            total += pltpu.roll(total, by, 0)
        ids = total[:1]
        bz, by = ids % 32, ids // 32 % 32
        mine[h : h + 1, :] = bz * 2048 + by * 64 + ids // 1024 % 64


def turn_unit(block, turned):
    def one(n, carry):
        part = block[pl.ds(n, 128, stride=16), :].T
        for u in range(2):
            for v in range(8):
                at = (u * 8 + v) * 8
                turned[n, pl.ds(u * 64 + v, 8, stride=8), :] = part[at : at + 8]
        return carry

    lax.fori_loop(0, 16, one, 0)


def y_group(g, data, hi, lo, table):
    lane = lax.broadcasted_iota(jnp.int32, (64, 128), 1)

    def four(p, carry):
        rows = []
        for k in range(4):
            turned = data[pl.ds(4 * p + k, 256, stride=8), :].T
            rows.append(jnp.concatenate([turned[:64], turned[64:]], 1))
        res = dot3(halves(jnp.concatenate(rows, 0)), (hi[...], lo[...]), ((1,), (0,)))
        for k in range(4):
            bz = 8 * g + 4 * p + k
            for high in range(4):
                part = res[k * 64 : (k + 1) * 64, high * 128 : (high + 1) * 128]
                for low in range(8):
                    source = low * 16 + jnp.bitwise_and(lane, 15)
                    at = pl.multiple_of((bz * 32 + high * 8 + low) * 64, 64)
                    table[pl.ds(at, 64), :] = jnp.take_along_axis(part, source, axis=1)
        return carry

    lax.fori_loop(0, 2, four, 0)


def pick_group(to, gx, rows, table, raw):
    owners = [(gx + g) % GX for g in range(8)]

    def eight(t, carry):
        h, first = t // 16, t % 16 * 8
        views = [rows.at[to, owners[g], h] for g in range(8)]
        for s in range(8):
            for g in range(8):
                lanes = slice(g * 16, g * 16 + 16)
                row = views[g][first + s]
                raw[pl.ds(t * 8 + s, 1), lanes] = table[pl.ds(row, 1), lanes]
        return carry

    lax.fori_loop(0, 32, eight, 0)


def spread_kernel(
    images, z_hi_in, z_lo_in, x_hi_in, x_lo_in, y_hi_in, y_lo_in, lists, slots, weights,
    out, turned_out,
    x_out, z_hi, z_lo, x_hi, x_lo, y_hi, y_lo, z_out, x_in, y_in, table, raw, rows_all, rows,
    near, near8, listed, mine, mine8, wide, block, turned,
    load_sem, self_sem, send1, recv1, send2, recv2, send3, recv3,
    small1, small2, small3, small4, block_sem, turned_sem, rows_sem,
):
    gx, gy = lax.axis_index("gx"), lax.axis_index("gy")
    me = gx * GY + gy
    image = x_out
    loads = [
        pltpu.make_async_copy(src, dst, load_sem.at[i])
        for i, (src, dst) in enumerate(
            [(z_hi_in, z_hi), (z_lo_in, z_lo)]
            + [
                (images.at[c, q, :, pl.ds(half * 128, 128)], image.at[half * 4 + c * 2 + q])
                for c in range(2)
                for q in range(2)
                for half in range(2)
            ]
            + [(x_hi_in, x_hi), (x_lo_in, x_lo), (y_hi_in, y_hi), (y_lo_in, y_lo)]
        )
    ]
    for load in loads:
        load.start()

    barrier = pltpu.get_barrier_semaphore()
    for r in range(1, GX):
        pl.semaphore_signal(barrier, inc=1, device_id={"gx": (gx + r) % GX})
    for r in range(1, GY):
        pl.semaphore_signal(barrier, inc=1, device_id={"gy": (gy + r) % GY})
    pl.semaphore_wait(barrier, GX + GY - 2)

    def over_x(m, r):
        to = (gx + r) % GX
        return pltpu.make_async_remote_copy(
            src_ref=z_out.at[m, to],
            dst_ref=x_in.at[m, gx],
            send_sem=send1.at[m, r],
            recv_sem=recv1.at[m, r],
            device_id={"gx": to},
        )

    def part_y(m, b):
        return y_in.at[m % 4, pl.ds(pl.multiple_of(b * 128 + m // 4 * 64, 64), 64)]

    def over_y(m, r):
        to = (gy + r) % GY
        return pltpu.make_async_remote_copy(
            src_ref=x_out.at[m, pl.ds(pl.multiple_of(to * 64, 64), 64)],
            dst_ref=part_y(m, gy),
            send_sem=send2.at[m, r],
            recv_sem=recv2.at[m, r],
            device_id={"gy": to},
        )

    def own_y(m):
        src = x_out.at[m, pl.ds(pl.multiple_of(gy * 64, 64), 64)]
        return pltpu.make_async_copy(src, part_y(m, gy), self_sem.at[m])

    def picked(i, g):
        return z_out.at[g, i // 4, pl.ds(pl.multiple_of(i % 4 * 32, 32), 32)]

    def over_all(i, g):
        return pltpu.make_async_remote_copy(
            src_ref=picked(i, g),
            dst_ref=out.at[me],
            send_sem=send3.at[i, g],
            recv_sem=recv3.at[i, g],
            device_id={"gx": (gx + g) % GX, "gy": (gy + i) % GY},
        )

    hop1 = hops((lambda to: lists, near.at[gx]), "gx", GX, small1)
    hop2 = hops((lambda to: near8, listed.at[gy]), "gy", GY, small2)
    hop3 = hops((lambda to: mine, mine8.at[gx]), "gx", GX, small3)
    hop4 = hops((lambda to: mine8, rows_all.at[gy]), "gy", GY, small4)
    to_scalars = pltpu.make_async_copy(rows_all, rows, rows_sem)
    own = pltpu.make_async_copy(picked(0, 0), out.at[me], self_sem.at[8])

    def fetch(j, slot):
        src = weights.at[j // 4, :, pl.ds(j % 4 * 128, 128)]
        return pltpu.make_async_copy(src, block.at[slot], block_sem.at[slot])

    def put(j, slot):
        dst = turned_out.at[j // 4, :, pl.ds(j % 4 * 128, 128), :]
        return pltpu.make_async_copy(turned.at[slot], dst, turned_sem.at[slot])

    def z_half(half):
        for c in range(2):
            if half == 0:
                for load in loads[2 + 4 * c : 6 + 4 * c]:
                    load.wait()

            def pair(yp, carry):
                z_pair(yp + 4 * half, c, image, z_hi, z_lo, z_out)
                return carry

            lax.fori_loop(0, 4, pair, 0)

    def send_x(half):
        def one(m, carry):
            for r in range(1, GX):
                over_x(m, r).start()
            return carry

        lax.fori_loop(4 * half, 4 * half + 4, one, 0)

    for hop in hop1:
        hop.start()
    near[gx] = lists[...]
    for load in loads[:2]:
        load.wait()
    z_half(0)
    send_x(0)
    z_half(1)
    send_x(1)
    for slot in range(2):
        fetch(slot, slot).start()
    for hop in hop1:
        hop.wait()
    lane = lax.broadcasted_iota(jnp.int32, (1, 128), 1)
    for a in range(GX):
        kept = jnp.zeros((1, 128), jnp.int32)
        for k in range(4):
            moved = pltpu.roll(near[a, k : k + 1, :], (128 + 16 * k - 16 * gx) % 128, 1)
            kept = jnp.where(lane // 16 == k, moved, kept)
        near8[a : a + 1, :] = kept
    for hop in hop2:
        hop.start()
    listed[gy] = near8[...]
    for load in loads[10:]:
        load.wait()

    def chunk(m, carry):
        slot = m % 2
        fetch(m, slot).wait()

        @pl.when(m > 1)
        def _():
            put(m - 2, slot).wait()

        turn_unit(block.at[slot], turned.at[slot])
        put(m, slot).start()

        @pl.when(m < 6)
        def _():
            fetch(m + 2, slot).start()

        x_in[m, gx] = z_out[m, gx]
        for r in range(1, GX):
            over_x(m, r).wait_recv()
        both = jnp.concatenate([x_in[m, a] for a in range(8)], 1)
        res = dot3(halves(both), (x_hi[...], x_lo[...]), ((1,), (0,)))
        for c in range(2):
            for u in range(8):
                at = (c * 8 + u) * 64
                x_out[m, at : at + 64] = res[
                    c * 64 : (c + 1) * 64, u * 128 : (u + 1) * 128
                ]
        for r in range(1, GY):
            over_y(m, r).start()
        own_y(m).start()

        @pl.when(m == 2)
        def _():
            for hop in hop2:
                hop.wait()
            wide[...] = jnp.zeros((16, 128), jnp.int32)
            wide[:, :16] = slots[...]
            own_rows(listed, wide, mine, gy)
            for hop in hop3:
                hop.start()
            mine8[gx] = mine[...]

        @pl.when(m == 4)
        def _():
            for hop in hop3:
                hop.wait()
            for hop in hop4:
                hop.start()
            rows_all[gy] = mine8[...]

        return carry

    lax.fori_loop(0, 8, chunk, 0)

    def group_y(k, carry):
        for m in (k, k + 4):
            own_y(m).wait()
            for r in range(1, GY):
                over_y(m, r).wait_recv()
        y_group(k, y_in.at[k], y_hi, y_lo, table)
        return carry

    def sent_x(m, carry):
        for r in range(1, GX):
            over_x(m, r).wait_send()
        return carry

    lax.fori_loop(0, 8, sent_x, 0)
    for hop in hop4:
        hop.wait()
    to_scalars.start()
    for slot in range(2):
        put(6 + slot, slot).wait()
    lax.fori_loop(0, 4, group_y, 0)
    to_scalars.wait()

    def group(i, carry):
        to = (gy + i) % GY
        pick_group(to, gx, rows, table, raw)
        for h in range(2):
            turned_raw = raw[h * 128 : (h + 1) * 128, :].T
            for g in range(8):
                at = pl.multiple_of(i % 4 * 32 + h * 16, 16)
                part = turned_raw[g * 16 : (g + 1) * 16]
                z_out[g, i // 4, pl.ds(at, 16), :] = part

        @pl.when(i == 0)
        def _():
            own.start()

        @pl.when(i > 0)
        def _():
            over_all(i, 0).start()

        for g in range(1, 8):
            over_all(i, g).start()
        return carry

    lax.fori_loop(0, 16, group, 0)
    own.wait()

    def finish(m, carry):
        for r in range(1, GY):
            over_y(m, r).wait_send()
        return carry

    lax.fori_loop(0, 8, finish, 0)

    def finish_all(i, carry):
        @pl.when(i > 0)
        def _():
            over_all(i, 0).wait()

        for g in range(1, 8):
            over_all(i, g).wait()
        return carry

    lax.fori_loop(0, 16, finish_all, 0)


def spread(images, lists, slots, weights):
    tables = [jnp.asarray(t) for t in z_table() + x_table() + y_table()]
    hbm = pl.BlockSpec(memory_space=pltpu.HBM)
    inside = pl.BlockSpec(memory_space=pltpu.VMEM)
    dma = pltpu.SemaphoreType.DMA
    i32 = jnp.int32
    return pl.pallas_call(
        spread_kernel,
        out_shape=(
            jax.ShapeDtypeStruct((DEVS, 32, 128), F32),
            jax.ShapeDtypeStruct((2, 16, 512, 128), F32),
        ),
        in_specs=[hbm] * 7 + [inside] * 2 + [hbm],
        out_specs=(hbm,) * 2,
        scratch_shapes=[
            pltpu.VMEM((8, 1024, 128), F32),
            pltpu.VMEM((256, 512), BF16),
            pltpu.VMEM((256, 512), BF16),
            pltpu.VMEM((1024, 1024), BF16),
            pltpu.VMEM((1024, 1024), BF16),
            pltpu.VMEM((512, 512), BF16),
            pltpu.VMEM((512, 512), BF16),
            pltpu.VMEM((8, 8, 128, 128), F32),
            pltpu.VMEM((8, 8, 128, 128), F32),
            pltpu.VMEM((4, 2048, 128), F32),
            pltpu.VMEM((65536, 128), F32),
            pltpu.VMEM((256, 128), F32),
            pltpu.VMEM((GY, GX, 2, 128), i32),
            pltpu.SMEM((GY, GX, 2, 128), i32),
            pltpu.VMEM((GX, 4, 128), i32),
            pltpu.VMEM((GX, 128), i32),
            pltpu.VMEM((GY, GX, 128), i32),
            pltpu.VMEM((2, 128), i32),
            pltpu.VMEM((GX, 2, 128), i32),
            pltpu.VMEM((16, 128), i32),
            pltpu.VMEM((2, 2048, 128), F32),
            pltpu.VMEM((2, 16, 128, 128), F32),
            dma((14,)),
            dma((9,)),
            dma((8, GX)),
            dma((8, GX)),
            dma((8, GY)),
            dma((8, GY)),
            dma((16, 8)),
            dma((16, 8)),
            dma((2, GX)),
            dma((2, GY)),
            dma((2, GX)),
            dma((2, GY)),
            dma((2,)),
            dma((2,)),
            dma,
        ],
        compiler_params=pltpu.CompilerParams(
            vmem_limit_bytes=WIDE_VMEM, collective_id=0, has_side_effects=True
        ),
        name="spread",
    )(images, *tables, lists, slots, weights)


def sum_kernel(got, weights, out):
    rows = []
    for half in range(2):

        def one(u, carry):
            sums = list(carry)
            for w in range(8):
                at = pl.multiple_of(u * 64 + w * 8, 8)
                factors = [weights[0, 4 * half + n, pl.ds(at, 8), :] for n in range(4)]
                for k in range(4):
                    value = got[w, k // 2, u, 0, k % 2]
                    for n in range(4):
                        sums[n * 4 + k] = sums[n * 4 + k] + factors[n] * value
            return tuple(sums)

        sums = lax.fori_loop(0, 8, one, (jnp.zeros((8, 128), F32),) * 16)
        rows += [jnp.sum(s, 0, keepdims=True) for s in sums]
    lane = lax.broadcasted_iota(jnp.int32, (8, 128), 1)
    owner = lax.broadcasted_iota(jnp.int32, (8, 128), 0)
    ones = jnp.where(lane // 16 == owner, 1.0, 0.0)
    out[0, 0] = lax.dot_general(
        ones,
        jnp.concatenate(rows, 0),
        (((1,), (1,)), ((), ())),
        precision=lax.Precision.HIGHEST,
        preferred_element_type=F32,
    )


def interpolate(got, weights):
    return pl.pallas_call(
        sum_kernel,
        out_shape=jax.ShapeDtypeStruct((2, 2, 8, 32), F32),
        grid=(2, 2),
        in_specs=[
            pl.BlockSpec((8, 2, 8, 1, 2, 8, 128), lambda h, n: (0, 0, 0, h, 0, 0, 0)),
            pl.BlockSpec((1, 8, 512, 128), lambda h, n: (h, n, 0, 0)),
        ],
        out_specs=pl.BlockSpec((1, 1, 8, 32), lambda h, n: (h, n, 0, 0)),
        compiler_params=pltpu.CompilerParams(vmem_limit_bytes=WIDE_VMEM),
        name="interpolate",
    )(got, weights)


def local(coil_images, send_lists, seg_slots, weights, counts):
    lists = send_lists[0].T
    got, turned = spread(
        coil_images.reshape(2, 2, 1024, 256),
        lists,
        seg_slots,
        weights.reshape(2, 2048, 512),
    )
    sums = interpolate(got.reshape(8, 2, 8, 2, 2, 8, 128), turned)
    samples = sums.reshape(2, 2, 8, 8, 2, 2).transpose(0, 2, 4, 5, 1, 3)
    samples = samples.reshape(16, 2, 2, 16)
    live = jnp.arange(16, dtype=jnp.int32) < counts[:, None, None, None]
    return jnp.where(live, samples, 0.0)


def solution(mesh):
    placed = (
        P(None, None, "gx", "gy", None),
        P(("gx", "gy"), None, None),
        P(("gx", "gy"), None),
        P(("gx", "gy"), None, None, None),
        P(("gx", "gy")),
    )
    return jax.shard_map(
        local,
        mesh=mesh,
        in_specs=placed,
        out_specs=P(("gx", "gy"), None, None, None),
        check_vma=False,
    )
```
